512 devices in a mesh: row: 32 (over x_hi, y, core), col: 16 (over z, x_lo).
Axes of the slice: x: 4 (x_hi: 2, x_lo: 2; x = x_hi * 2 + x_lo), y: 8, z: 8, core: 2. Of those that a mesh axis runs over, the one named last changes fastest.
Arguments:
- schur_tile: float32 [8192, 8192], P('row', 'col'), may hold values from -2 to 6, as said below
- swap_mask: int32 [2, 32], P(None, 'row'), may hold values from 0 to 1, as said below
Outputs:
- reordered: float32 [8192, 8192], P('row', 'col')
The draws below stay inside these ranges and needn't reach their ends.
Inputs may be any that keep to these rules, and one draw needn't show every extreme that they name: schur_tile is upper triangular; the diagonal entries of rows j * 128 to j * 128 + 127 lie within 0.15 of 0.75 + 1.5 (j mod 4). swap_mask[1, 31] is 0.
All inputs are finite; a program needn't handle non-finite values.
Results may differ from the reference program's by a relative error of at most 0.0003.
Values sent between devices are 32-bit elements; how exact they have to be, the bound alone decides.
No kernel may reach another device: no remote copies, remote signals or barrier semaphores. Data moves between devices by JAX's collectives and lax.ppermute only.
A program may use at most 64 MiB of HBM per device.

```python
import math
import jax
import jax.numpy as jnp
from jax import lax

K = 128
DOUBLINGS = 2
W = 8192
NP = 32


def draw_schur_tile(key, part):
    positions = jnp.arange(W, dtype=jnp.int32)
    cluster = positions // K
    levels = 0.75 + 1.5 * (cluster % 4).astype(jnp.float32)
    key_diag, key_off = jax.random.split(key, 2)
    spread = jax.random.uniform(key_diag, (W,), jnp.float32, -0.15, 0.15)
    noise_field = jnp.clip(jax.random.normal(key_off, (W, W), jnp.float32), -6.0, 6.0)
    row_cluster = cluster[:, None]
    col_cluster = cluster[None, :]
    above_band = row_cluster < col_cluster
    inside = (row_cluster == col_cluster) & (positions[:, None] < positions[None, :])
    entry_scale = jnp.where(above_band, 1.0, jnp.where(inside, 0.1, 0.0)) / math.sqrt(K)
    result_tile = noise_field * entry_scale + jnp.diag(levels + spread)
    return result_tile.astype(jnp.float32)


def draw_swap_mask(key, part):
    swap_flags = jax.random.randint(key, (2, NP), 0, 2, dtype=jnp.int32)
    return swap_flags.at[1, NP - 1].set(0)


def setup_inputs(seed: int = 0) -> dict:
    seeds = jax.random.split(jax.random.key(seed), 3)
    return {
        "schur_tile": draw_schur_tile(jax.random.fold_in(seeds[2], 71), 0),
        "swap_mask": draw_swap_mask(jax.random.fold_in(seeds[2], 71), 0),
    }


precise = lax.Precision.HIGHEST

def product(left_matrix, right_matrix):
    return jnp.matmul(left_matrix, right_matrix, precision=precise)

def swap_factor(pair_block, swap_flag):
    half_order = pair_block.shape[0] // 2
    upper_block = pair_block[:half_order, :half_order]
    lower_block = pair_block[half_order:, half_order:]
    coupling = pair_block[:half_order, half_order:]
    identity = jnp.eye(half_order, dtype=pair_block.dtype)
    center = jnp.trace(lower_block) / half_order
    shifted_upper = upper_block - center * identity
    normal_matrix = product(shifted_upper.T, shifted_upper)
    low_factor = jnp.linalg.cholesky(normal_matrix)
    left_inverse = jax.scipy.linalg.cho_solve((low_factor, True), shifted_upper.T)
    right_operator = lower_block - center * identity
    solution = product(left_inverse, coupling)
    for doubling in range(DOUBLINGS):
        solution = solution + product(left_inverse, product(solution, right_operator))
        if doubling + 1 < DOUBLINGS:
            left_inverse = product(left_inverse, left_inverse)
            right_operator = product(right_operator, right_operator)
    gram_one = identity + product(solution.T, solution)
    gram_two = identity + product(solution, solution.T)
    low_one = jnp.linalg.cholesky(gram_one)
    low_two = jnp.linalg.cholesky(gram_two)
    top_rows = jax.scipy.linalg.solve_triangular(low_one, jnp.concatenate([-solution.T, identity], axis=1), lower=True)
    bottom_rows = jax.scipy.linalg.solve_triangular(low_two, jnp.concatenate([identity, solution], axis=1), lower=True)
    swapped = jnp.concatenate([top_rows, bottom_rows], axis=0)
    return jnp.where(swap_flag > 0, swapped, jnp.eye(2 * half_order, dtype=pair_block.dtype))

def apply_round(matrix, swap_flags):
    matrix_order = matrix.shape[0]
    pair_width = 2 * K
    pair_count = matrix_order // pair_width

    def one_pair(pair_index):
        start_row = (pair_index * pair_width).astype(jnp.int32)
        pair_block = lax.dynamic_slice(matrix, (start_row, start_row), (pair_width, pair_width))
        return swap_factor(pair_block, swap_flags[pair_index])
    factors = lax.map(one_pair, jnp.arange(pair_count, dtype=jnp.int32))
    rows_view = matrix.reshape(pair_count, pair_width, matrix_order)
    left_done = jnp.einsum('pkl,plw->pkw', factors, rows_view, precision=precise).reshape(matrix_order, matrix_order)
    cols_view = left_done.reshape(matrix_order, pair_count, pair_width)
    return jnp.einsum('wpk,plk->wpl', cols_view, factors, precision=precise).reshape(matrix_order, matrix_order)

def reference(schur_tile, swap_mask):
    after_first = apply_round(schur_tile, swap_mask[0])
    shifted = jnp.roll(after_first, (-K, -K), axis=(0, 1))
    second = apply_round(shifted, swap_mask[1])
    return jnp.roll(second, (K, K), axis=(0, 1))
```

```python
import jax
import jax.numpy as jnp
from jax import lax
from jax.sharding import PartitionSpec as P

K = 128
DOUBLINGS = 2


precise = lax.Precision.HIGHEST
AXES = ("row", "col")


def shifted_2(value, axis, steps):
    count = lax.axis_size(axis)
    pairs = [(source, (source + steps) % count) for source in range(count)]
    return lax.ppermute(value, axis, pairs)


def product(left_matrix, right_matrix):
    return jnp.matmul(left_matrix, right_matrix, precision=precise)


def swap_factor(pair_block, swap_flag):
    half_order = pair_block.shape[0] // 2
    upper_block = pair_block[:half_order, :half_order]
    lower_block = pair_block[half_order:, half_order:]
    coupling = pair_block[:half_order, half_order:]
    identity = jnp.eye(half_order, dtype=pair_block.dtype)
    center = jnp.trace(lower_block) / half_order
    shifted_upper = upper_block - center * identity
    normal_matrix = product(shifted_upper.T, shifted_upper)
    low_factor = jnp.linalg.cholesky(normal_matrix)
    left_inverse = jax.scipy.linalg.cho_solve((low_factor, True), shifted_upper.T)
    right_operator = lower_block - center * identity
    solution = product(left_inverse, coupling)
    for doubling in range(DOUBLINGS):
        solution = solution + product(left_inverse, product(solution, right_operator))
        if doubling + 1 < DOUBLINGS:
            left_inverse = product(left_inverse, left_inverse)
            right_operator = product(right_operator, right_operator)
    gram_one = identity + product(solution.T, solution)
    gram_two = identity + product(solution, solution.T)
    low_one = jnp.linalg.cholesky(gram_one)
    low_two = jnp.linalg.cholesky(gram_two)
    top_rows = jax.scipy.linalg.solve_triangular(
        low_one, jnp.concatenate([-solution.T, identity], axis=1), lower=True
    )
    bottom_rows = jax.scipy.linalg.solve_triangular(
        low_two, jnp.concatenate([identity, solution], axis=1), lower=True
    )
    swapped = jnp.concatenate([top_rows, bottom_rows], axis=0)
    return jnp.where(swap_flag > 0, swapped, jnp.eye(2 * half_order, dtype=pair_block.dtype))


def trees(own):
    cols = lax.axis_size("col")
    at = lambda r, c: r * cols + c
    sign = lambda r: 1 - 2 * (r % 2)
    row_value = own
    col_value = own
    sources = [0]
    step = cols // 2
    while step:
        row_pairs = [
            (at(r, (r // 2 + sign(r) * s) % cols), at(r, (r // 2 + sign(r) * (s + step)) % cols))
            for r in range(2 * cols)
            for s in sources
        ]
        col_pairs = [
            (at(2 * ((c + sign(k) * s) % cols) + k, c), at(2 * ((c + sign(k) * (s + step)) % cols) + k, c))
            for c in range(cols)
            for k in range(2)
            for s in sources
        ]
        row_in = lax.ppermute(row_value, AXES, row_pairs)
        col_in = lax.ppermute(col_value, AXES, col_pairs)
        row_value = row_value + row_in
        col_value = col_value + col_in
        sources = sources + [s + step for s in sources]
        step //= 2
    swap = [
        (at(2 * q + k, c), at(2 * q + 1 - k, c))
        for c in range(cols)
        for q in range(cols)
        for k in range(2)
    ]
    other = lax.ppermute(col_value, AXES, swap)
    odd = lax.axis_index("row") % 2 == 1
    return row_value, jnp.where(odd, other, col_value), jnp.where(odd, col_value, other)


def round_update(matrix, swap_flags):
    row_index = lax.axis_index("row")
    col_index = lax.axis_index("col")
    odd = row_index % 2 == 1
    owner = col_index == row_index // 2
    block = jnp.where(odd, matrix[:, 2 * K :], matrix[:, : 2 * K])
    factor = jnp.where(owner, swap_factor(block, swap_flags[0]), 0.0)
    row_factor, even_factor, odd_factor = trees(factor)
    col_factors = jnp.stack([even_factor, odd_factor])
    cols_view = matrix.reshape(matrix.shape[0], -1, 2 * K)
    current = jnp.einsum("wpk,plk->wpl", cols_view, col_factors, precision=precise).reshape(
        matrix.shape
    )
    return product(row_factor, current)


def body(schur_tile, swap_mask):
    after_first = round_update(schur_tile, swap_mask[0])
    top_strip = after_first[:K]
    from_below = shifted_2(top_strip, "row", -1)
    rows_moved = jnp.concatenate([after_first[K:], from_below], axis=0)
    left_strip = rows_moved[:, :K]
    from_right = shifted_2(left_strip, "col", -1)
    shifted = jnp.concatenate([rows_moved[:, K:], from_right], axis=1)
    second = round_update(shifted, swap_mask[1])
    right_strip = second[:, second.shape[1] - K :]
    from_left = shifted_2(right_strip, "col", 1)
    cols_back = jnp.concatenate([from_left, second[:, : second.shape[1] - K]], axis=1)
    bottom_strip = cols_back[cols_back.shape[0] - K :]
    from_above = shifted_2(bottom_strip, "row", 1)
    return jnp.concatenate([from_above, cols_back[: cols_back.shape[0] - K]], axis=0)


def solution(mesh):
    placed = (P("row", "col"), P(None, "row"))
    return jax.shard_map(
        body, mesh=mesh, in_specs=placed, out_specs=P("row", "col"), check_vma=False
    )
```

```python
import jax
import jax.numpy as jnp
from jax import lax
from jax.experimental import pallas as pl
from jax.experimental.pallas import tpu as pltpu
from jax.sharding import PartitionSpec as P

K = 128
DOUBLINGS = 2


precise = lax.Precision.HIGHEST
AXES = ("row", "col")


def shifted_2(value, axis, steps):
    count = lax.axis_size(axis)
    pairs = [(source, (source + steps) % count) for source in range(count)]
    return lax.ppermute(value, axis, pairs)


def product(left_matrix, right_matrix):
    return jnp.matmul(left_matrix, right_matrix, precision=precise)


NN=((1,),(0,)); NT=((1,),(1,))

def halves(x):
    hi = x.astype(jnp.bfloat16)
    return hi, (x - hi.astype(jnp.float32)).astype(jnp.bfloat16)

def dot1(a, b, dims):
    return lax.dot_general(a, b, (dims, ((), ())), preferred_element_type=jnp.float32)

def mm(a, b, dims=NN):
    ah, al = halves(a); bh, bl = halves(b)
    return dot1(ah, bh, dims) + (dot1(ah, bl, dims) + dot1(al, bh, dims))

def mlow(a, b, dims=NN):
    return dot1(a.astype(jnp.bfloat16), b.astype(jnp.bfloat16), dims)

def grids():
    i = lax.broadcasted_iota(jnp.int32, (K, K), 0)
    j = lax.broadcasted_iota(jnp.int32, (K, K), 1)
    return (i == j).astype(jnp.float32), jnp.where(i > j, 1.0, jnp.where(i == j, 0.5, 0.0))

def worst(parts):
    sums = [jnp.sum(x * x) for x in parts]
    top = sums[0]
    for value in sums[1:]:
        top = jnp.where(value <= top, top, value)
    return top

def fast_inverse_cholesky(s_list, eye, phi):
    n = len(s_list)
    ws = []
    for s in s_list:
        d = s * eye
        dr = lax.rsqrt(jnp.sum(d, axis=0, keepdims=True)); dc = lax.rsqrt(jnp.sum(d, axis=1, keepdims=True))
        ws.append((s * dc * dr - eye, dr))
    ps = [phi * e for e, _ in ws]
    qs = [mlow(p, p, NT) for p in ps]
    ps = [phi * (e - q) for (e, _), q in zip(ws, qs)]
    qs = [mlow(p, p) for p in ps]
    w = [(eye - p + q) * dr for p, q, (_, dr) in zip(ps, qs, ws)]
    for last in range(2):
        dot = mm if last else mlow
        t = [dot(a, s) for a, s in zip(w, s_list)]
        e = [dot(a, b, NT) - eye for a, b in zip(t, w)]
        u = [dot(phi * b, a) for a, b in zip(w, e)]
        w = [a - b for a, b in zip(w, u)]
    return w, worst(e)

def fast_inverse(a_list, eye):
    cs = [K / jnp.sum(a * eye) for a in a_list]
    r = [eye - a * c for a, c in zip(a_list, cs)]
    r2 = [mm(x, x) for x in r]
    pa = [eye + x for x in r]
    r4 = [mm(x, x) for x in r2]
    pa = [p + mm(q, p) for p, q in zip(pa, r2)]
    return [(p + mm(q, p)) * c for p, q, c in zip(pa, r4, cs)], worst(r4)

def finish(m, c, nop):
    x = [mm(a, b) for a, b in zip(m, c)]
    t = [mm(a, b) for a, b in zip(x, nop)]
    m2 = [mm(a, a) for a in m]
    n2 = [mm(a, a) for a in nop]
    x = [a + mm(b, q) for a, b, q in zip(x, m, t)]
    t = [mm(a, b) for a, b in zip(x, n2)]
    return [a + mm(b, q) for a, b, q in zip(x, m2, t)]

def direct_inverse_cholesky(s):
    i = lax.broadcasted_iota(jnp.int32, (K, K), 0)
    i2 = lax.broadcasted_iota(jnp.int32, (K, 2 * K), 0)
    j2 = lax.broadcasted_iota(jnp.int32, (K, 2 * K), 1)
    t0 = jnp.concatenate([s, (i == lax.broadcasted_iota(jnp.int32, (K, K), 1)).astype(jnp.float32)], axis=1)
    def step(j, t):
        row = jnp.sum(jnp.where(i2 == j, t, 0.0), axis=0, keepdims=True)
        col = jnp.sum(jnp.where(j2 == j, t, 0.0), axis=1, keepdims=True)
        piv = jnp.sum(jnp.where(j2[:1] == j, row, 0.0), axis=1, keepdims=True)
        new = row * lax.rsqrt(piv)
        t = t - jnp.where(i2 > j, col * lax.rsqrt(piv), 0.0) * new
        return jnp.where(i2 == j, new, t)
    return lax.fori_loop(0, K, step, t0)[:, K:]

def pair_factors(a_list, c_list, b_list, out_refs, flags):
    eye, phi = grids()
    shifts = [jnp.sum(b * eye) / K for b in b_list]
    on = [f > 0 for f in flags]
    a_s = [jnp.where(f, a - s * eye, eye) for f, a, s in zip(on, a_list, shifts)]
    c_list = [jnp.where(f, c, 0.0) for f, c in zip(on, c_list)]
    nop = [jnp.where(f, b - s * eye, 0.0) for f, b, s in zip(on, b_list, shifts)]
    m, e0 = fast_inverse(a_s, eye)
    def rest(m, chol):
        x = finish(m, c_list, nop)
        xt = [v.T for v in x]
        grams = [eye + mm(v, v, NT) for v in xt] + [eye + mm(v, v, NT) for v in x]
        w, e1 = chol(grams)
        n = len(x)
        for p in range(n):
            w1, w2 = w[p], w[n + p]
            keep = on[p]
            out_refs[p][:K, :K] = jnp.where(keep, -mm(w1, xt[p]), eye)
            out_refs[p][:K, K:] = jnp.where(keep, w1, 0.0)
            out_refs[p][K:, :K] = jnp.where(keep, w2, 0.0)
            out_refs[p][K:, K:] = jnp.where(keep, mm(w2, x[p]), eye)
        return e1
    e1 = rest(m, lambda g: fast_inverse_cholesky(g, eye, phi))
    good = jnp.logical_and(e0 < 1e-5, e1 < 6e-3)
    @pl.when(jnp.logical_not(good))
    def _():
        inv = []
        for a in a_s:
            at = a.T
            w = direct_inverse_cholesky(mm(at, at, NT))
            inv.append(mm(mm(w.T, w.T, NT), at))
        rest(inv, lambda g: ([direct_inverse_cholesky(v) for v in g], jnp.float32(0)))

def factor_kernel(flag_ref, block_ref, out_ref):
    @pl.when(flag_ref[1] == 0)
    def _():
        out_ref[...] = jnp.zeros_like(out_ref)

    @pl.when(flag_ref[1] > 0)
    def _():
        pair_factors([block_ref[:K, :K]], [block_ref[:K, K:]], [block_ref[K:, K:]], [out_ref], [flag_ref[0]])


def owned_factor(block, flag, owner):
    return pl.pallas_call(
        factor_kernel,
        out_shape=jax.ShapeDtypeStruct((2 * K, 2 * K), jnp.float32),
        in_specs=[pl.BlockSpec(memory_space=pltpu.SMEM), pl.BlockSpec(memory_space=pltpu.VMEM)],
        out_specs=pl.BlockSpec(memory_space=pltpu.VMEM),
        name="factor",
    )(jnp.stack([flag, owner.astype(jnp.int32)]), block)


def trees(own):
    cols = lax.axis_size("col")
    at = lambda r, c: r * cols + c
    sign = lambda r: 1 - 2 * (r % 2)
    row_value = own
    col_value = own
    orders = ((8, 4, 2, 1), (1, 8, 4, 2))
    sources = [[0], [0]]
    for i in range(4):
        row_pairs = [
            (at(r, (r // 2 + sign(r) * s) % cols), at(r, (r // 2 + sign(r) * (s + orders[r % 2][i])) % cols))
            for r in range(2 * cols)
            for s in sources[r % 2]
        ]
        col_pairs = [
            (at(2 * ((c + sign(k) * s) % cols) + k, c), at(2 * ((c + sign(k) * (s + orders[k][i])) % cols) + k, c))
            for c in range(cols)
            for k in range(2)
            for s in sources[k]
        ]
        row_in = lax.ppermute(row_value, AXES, row_pairs)
        col_in = lax.ppermute(col_value, AXES, col_pairs)
        row_value = row_value + row_in
        col_value = col_value + col_in
        sources = [s + [v + orders[k][i] for v in s] for k, s in enumerate(sources)]
    swap = [
        (at(2 * q + k, c), at(2 * q + 1 - k, c))
        for c in range(cols)
        for q in range(cols)
        for k in range(2)
    ]
    other = lax.ppermute(col_value, AXES, swap)
    odd = lax.axis_index("row") % 2 == 1
    return row_value, jnp.where(odd, other, col_value), jnp.where(odd, col_value, other)


def round_update(matrix, swap_flags):
    row_index = lax.axis_index("row")
    col_index = lax.axis_index("col")
    odd = row_index % 2 == 1
    owner = col_index == row_index // 2
    block = jnp.where(odd, matrix[:, 2 * K :], matrix[:, : 2 * K])
    factor = owned_factor(block, swap_flags[0], owner)
    row_factor, even_factor, odd_factor = trees(factor)
    col_factors = jnp.stack([even_factor, odd_factor])
    cols_view = matrix.reshape(matrix.shape[0], -1, 2 * K)
    current = jnp.einsum("wpk,plk->wpl", cols_view, col_factors, precision=precise).reshape(
        matrix.shape
    )
    return product(row_factor, current)


def body(schur_tile, swap_mask):
    after_first = round_update(schur_tile, swap_mask[0])
    top_strip = after_first[:K]
    from_below = shifted_2(top_strip, "row", -1)
    rows_moved = jnp.concatenate([after_first[K:], from_below], axis=0)
    left_strip = rows_moved[:, :K]
    from_right = shifted_2(left_strip, "col", -1)
    shifted = jnp.concatenate([rows_moved[:, K:], from_right], axis=1)
    second = round_update(shifted, swap_mask[1])
    right_strip = second[:, second.shape[1] - K :]
    from_left = shifted_2(right_strip, "col", 1)
    cols_back = jnp.concatenate([from_left, second[:, : second.shape[1] - K]], axis=1)
    bottom_strip = cols_back[cols_back.shape[0] - K :]
    from_above = shifted_2(bottom_strip, "row", 1)
    return jnp.concatenate([from_above, cols_back[: cols_back.shape[0] - K]], axis=0)


def solution(mesh):
    placed = (P("row", "col"), P(None, "row"))
    return jax.shard_map(
        body, mesh=mesh, in_specs=placed, out_specs=P("row", "col"), check_vma=False
    )
```

```python
import jax
import jax.numpy as jnp
from jax import lax
from jax.experimental import pallas as pl
from jax.experimental.pallas import tpu as pltpu
from jax.sharding import PartitionSpec as P

K = 128
DOUBLINGS = 2


AXES = ("row", "col")


NN=((1,),(0,)); NT=((1,),(1,))

def halves(x):
    hi = x.astype(jnp.bfloat16)
    return hi, (x - hi.astype(jnp.float32)).astype(jnp.bfloat16)

def dot1(a, b, dims):
    return lax.dot_general(a, b, (dims, ((), ())), preferred_element_type=jnp.float32)

def mm(a, b, dims=NN):
    ah, al = halves(a); bh, bl = halves(b)
    return dot1(ah, bh, dims) + (dot1(ah, bl, dims) + dot1(al, bh, dims))

def mlow(a, b, dims=NN):
    return dot1(a.astype(jnp.bfloat16), b.astype(jnp.bfloat16), dims)

def grids():
    i = lax.broadcasted_iota(jnp.int32, (K, K), 0)
    j = lax.broadcasted_iota(jnp.int32, (K, K), 1)
    return (i == j).astype(jnp.float32), jnp.where(i > j, 1.0, jnp.where(i == j, 0.5, 0.0))

def worst(parts):
    sums = [jnp.sum(x * x) for x in parts]
    top = sums[0]
    for value in sums[1:]:
        top = jnp.where(value <= top, top, value)
    return top

def fast_inverse_cholesky(s_list, eye, phi):
    n = len(s_list)
    ws = []
    for s in s_list:
        d = s * eye
        dr = lax.rsqrt(jnp.sum(d, axis=0, keepdims=True)); dc = lax.rsqrt(jnp.sum(d, axis=1, keepdims=True))
        ws.append((s * dc * dr - eye, dr))
    ps = [phi * e for e, _ in ws]
    qs = [mlow(p, p, NT) for p in ps]
    ps = [phi * (e - q) for (e, _), q in zip(ws, qs)]
    qs = [mlow(p, p) for p in ps]
    w = [(eye - p + q) * dr for p, q, (_, dr) in zip(ps, qs, ws)]
    for last in range(2):
        dot = mm if last else mlow
        t = [dot(a, s) for a, s in zip(w, s_list)]
        e = [dot(a, b, NT) - eye for a, b in zip(t, w)]
        u = [dot(phi * b, a) for a, b in zip(w, e)]
        w = [a - b for a, b in zip(w, u)]
    return w, worst(e)

def fast_inverse(a_list, eye):
    cs = [K / jnp.sum(a * eye) for a in a_list]
    r = [eye - a * c for a, c in zip(a_list, cs)]
    r2 = [mm(x, x) for x in r]
    pa = [eye + x for x in r]
    r4 = [mm(x, x) for x in r2]
    pa = [p + mm(q, p) for p, q in zip(pa, r2)]
    return [(p + mm(q, p)) * c for p, q, c in zip(pa, r4, cs)], worst(r4)

def finish(m, c, nop):
    x = [mm(a, b) for a, b in zip(m, c)]
    t = [mm(a, b) for a, b in zip(x, nop)]
    m2 = [mm(a, a) for a in m]
    n2 = [mm(a, a) for a in nop]
    x = [a + mm(b, q) for a, b, q in zip(x, m, t)]
    t = [mm(a, b) for a, b in zip(x, n2)]
    return [a + mm(b, q) for a, b, q in zip(x, m2, t)]

def direct_inverse_cholesky(s):
    i = lax.broadcasted_iota(jnp.int32, (K, K), 0)
    i2 = lax.broadcasted_iota(jnp.int32, (K, 2 * K), 0)
    j2 = lax.broadcasted_iota(jnp.int32, (K, 2 * K), 1)
    t0 = jnp.concatenate([s, (i == lax.broadcasted_iota(jnp.int32, (K, K), 1)).astype(jnp.float32)], axis=1)
    def step(j, t):
        row = jnp.sum(jnp.where(i2 == j, t, 0.0), axis=0, keepdims=True)
        col = jnp.sum(jnp.where(j2 == j, t, 0.0), axis=1, keepdims=True)
        piv = jnp.sum(jnp.where(j2[:1] == j, row, 0.0), axis=1, keepdims=True)
        new = row * lax.rsqrt(piv)
        t = t - jnp.where(i2 > j, col * lax.rsqrt(piv), 0.0) * new
        return jnp.where(i2 == j, new, t)
    return lax.fori_loop(0, K, step, t0)[:, K:]

def pair_factors(a_list, c_list, b_list, out_refs, flags):
    eye, phi = grids()
    shifts = [jnp.sum(b * eye) / K for b in b_list]
    on = [f > 0 for f in flags]
    a_s = [jnp.where(f, a - s * eye, eye) for f, a, s in zip(on, a_list, shifts)]
    c_list = [jnp.where(f, c, 0.0) for f, c in zip(on, c_list)]
    nop = [jnp.where(f, b - s * eye, 0.0) for f, b, s in zip(on, b_list, shifts)]
    m, e0 = fast_inverse(a_s, eye)
    def rest(m, chol):
        x = finish(m, c_list, nop)
        xt = [v.T for v in x]
        grams = [eye + mm(v, v, NT) for v in xt] + [eye + mm(v, v, NT) for v in x]
        w, e1 = chol(grams)
        n = len(x)
        for p in range(n):
            w1, w2 = w[p], w[n + p]
            keep = on[p]
            out_refs[p][:K, :K] = jnp.where(keep, -mm(w1, xt[p]), eye)
            out_refs[p][:K, K:] = jnp.where(keep, w1, 0.0)
            out_refs[p][K:, :K] = jnp.where(keep, w2, 0.0)
            out_refs[p][K:, K:] = jnp.where(keep, mm(w2, x[p]), eye)
        return e1
    e1 = rest(m, lambda g: fast_inverse_cholesky(g, eye, phi))
    good = jnp.logical_and(e0 < 1e-5, e1 < 6e-3)
    @pl.when(jnp.logical_not(good))
    def _():
        inv = []
        for a in a_s:
            at = a.T
            w = direct_inverse_cholesky(mm(at, at, NT))
            inv.append(mm(mm(w.T, w.T, NT), at))
        rest(inv, lambda g: ([direct_inverse_cholesky(v) for v in g], jnp.float32(0)))


def pick(odd, when_odd, when_even):
    return jnp.where(odd, when_odd, when_even)


def prepare_kernel(mask_ref, tile_ref, whole_ref, left_ref, own_ref):
    odd = lax.axis_index("row") % 2 == 1
    i = lax.broadcasted_iota(jnp.int32, (8, K), 0)
    j = lax.broadcasted_iota(jnp.int32, (8, K), 1)
    first = (mask_ref[0, 0] > 0).astype(jnp.float32)
    second = (mask_ref[1, 0] > 0).astype(jnp.float32)
    flags = jnp.where(j == 0, jnp.where(i == 7, first, jnp.where(i == 6, second, 0.0)), 0.0)
    whole_ref[...] = tile_ref[...]
    whole_ref[2 * K - 8 :, :K] = flags
    left_ref[...] = tile_ref[:, : 2 * K]
    own_ref[...] = pick(odd, tile_ref[:, 2 * K :], tile_ref[:, : 2 * K])
    own_ref[2 * K - 8 :, :K] = flags


def flags_of(ref):
    corner = ref[2 * K - 8 :, :K]
    i = lax.broadcasted_iota(jnp.int32, (8, K), 0)
    return jnp.sum(jnp.where(i == 7, corner, 0.0)) > 0.5, jnp.sum(jnp.where(i == 6, corner, 0.0)) > 0.5


def steps_kernel(mask_ref, tile_ref, partner_ref, above_ref, right_ref, next_ref, row_ref, col_ref, f1, f2):
    row = lax.axis_index("row")
    col = lax.axis_index("col")
    odd = row % 2 == 1
    owner = col == row // 2

    @pl.when(jnp.logical_not(owner))
    def _():
        row_ref[...] = jnp.zeros_like(row_ref)
        col_ref[...] = jnp.zeros_like(col_ref)

    @pl.when(owner)
    def _():
        W = 2 * K
        d0 = lambda i, j: pick(odd, tile_ref[i, W + j.start : W + j.stop], tile_ref[i, j])
        dm = lambda i, j: pick(odd, partner_ref[i, j], next_ref[i, j])
        dp = lambda i, j: pick(odd, next_ref[i, j], partner_ref[i, W + j.start : W + j.stop])
        lo, hi, full = slice(0, K), slice(K, W), slice(0, W)
        partner1, partner2 = flags_of(partner_ref)
        next1, next2 = flags_of(next_ref)
        odd_i = odd.astype(jnp.int32)
        p1, p2, n1, n2 = [v.astype(jnp.int32) for v in (partner1, partner2, next1, next2)]
        m_flag = odd_i * p1 + (1 - odd_i) * n1
        m_flag2 = odd_i * p2 + (1 - odd_i) * n2
        p_flag = odd_i * n1 + (1 - odd_i) * p1
        blocks = (dm, d0, dp)
        pair_factors(
            [d(lo, lo) for d in blocks],
            [d(lo, hi) for d in blocks],
            [d(hi, hi) for d in blocks],
            [f1.at[p] for p in range(3)],
            [m_flag, mask_ref[0, 0], p_flag],
        )

        def congruent(f, d):
            left, right = f[:, :K], f[:, K:]
            g = jnp.concatenate([mm(left, d(lo, lo)), mm(left, d(lo, hi)) + mm(right, d(hi, hi))], axis=1)
            return mm(g, f, NT)

        am = pick(odd, partner_ref[:, W:], above_ref[...])
        a0 = pick(odd, right_ref[...], tile_ref[:, W:])
        fm_low, f0_top, f0_low, fp_top = f1[0, K:, :], f1[1, :K, :], f1[1, K:, :], f1[2, :K, :]
        pair_factors(
            [congruent(fm_low, dm), congruent(f0_low, d0)],
            [mm(mm(fm_low, am), f0_top, NT), mm(mm(f0_low, a0), fp_top, NT)],
            [congruent(f0_top, d0), congruent(fp_top, dp)],
            [f2.at[p] for p in range(2)],
            [m_flag2, mask_ref[1, 0]],
        )
        for n, value in enumerate(
            (
                mm(f2[0, K:, :K], fm_low),
                mm(f2[0, K:, K:], f0_top),
                mm(f2[1, :K, :K], f0_low),
                mm(f2[1, :K, K:], fp_top),
            )
        ):
            row_ref[n * K : (n + 1) * K, :] = value
            col_ref[n * K : (n + 1) * K, :] = value


def rows_kernel(step_ref, up_ref, own_ref, down_ref, left_ref, right_ref):
    p1, p2, p3, p4 = [step_ref[n * K : (n + 1) * K, :] for n in range(4)]
    for half, out in ((slice(0, 2 * K), left_ref), (slice(2 * K, 4 * K), right_ref)):
        out[:K, :] = mm(p1, up_ref[:, half]) + mm(p2, own_ref[:, half])
        out[K:, :] = mm(p3, own_ref[:, half]) + mm(p4, down_ref[:, half])


def cols_kernel(mine_ref, other_ref, before_ref, left_ref, right_ref, after_ref, out_ref):
    odd = lax.axis_index("row") % 2 == 1
    part = lambda n, a, b: pick(odd, a[n * K : (n + 1) * K, :], b[n * K : (n + 1) * K, :])
    even = [part(n, other_ref, mine_ref) for n in range(4)]
    odds = [part(n, mine_ref, other_ref) for n in range(4)]
    before, left, right, after = before_ref[...], left_ref[...], right_ref[...], after_ref[...]
    out_ref[:, :K] = mm(before, even[0], NT) + mm(left, even[1], NT)
    out_ref[:, K : 2 * K] = mm(left, even[2], NT) + mm(right, even[3], NT)
    out_ref[:, 2 * K : 3 * K] = mm(left, odds[0], NT) + mm(right, odds[1], NT)
    out_ref[:, 3 * K :] = mm(right, odds[2], NT) + mm(after, odds[3], NT)


def local(kernel, shapes, args, name, scratch=(), masks=0):
    smem = pl.BlockSpec(memory_space=pltpu.SMEM)
    vmem = pl.BlockSpec(memory_space=pltpu.VMEM)
    return pl.pallas_call(
        kernel,
        out_shape=[jax.ShapeDtypeStruct(shape, jnp.float32) for shape in shapes],
        in_specs=[smem] * masks + [vmem] * (len(args) - masks),
        out_specs=[vmem] * len(shapes),
        scratch_shapes=list(scratch),
        name=name,
    )(*args)


def trees(row_value, col_value, cols):
    at = lambda r, c: r * cols + c
    row_lists = [
        [at(r, c) for c in range(r // 2, cols)] + ([at(r, r // 2 - 1)] if r % 2 == 0 and r else [])
        for r in range(2 * cols)
    ]
    col_lists = [
        [at(2 * q + k, c) for q in range(c, -1, -1)] + ([at(2 * c + 2 + k, c)] if c + 1 < cols else [])
        for k in range(2)
        for c in range(cols)
    ]
    orders = ((8, 4, 2, 1), (1, 8, 4, 2))
    sources = [[0], [0]]

    def pairs(lists, core, i):
        step = orders[core][i]
        return [(line[s], line[s + step]) for line in lists for s in sources[core] if s + step < len(line)]

    for i in range(4):
        row_in = lax.ppermute(row_value, AXES, pairs(row_lists[::2], 0, i) + pairs(row_lists[1::2], 1, i))
        col_in = lax.ppermute(col_value, AXES, pairs(col_lists[:cols], 0, i) + pairs(col_lists[cols:], 1, i))
        row_value, col_value = lax.optimization_barrier((row_value + row_in, col_value + col_in))
        sources = [s + [v + orders[k][i] for v in s] for k, s in enumerate(sources)]
    swap = [(at(2 * q + k, c), at(2 * q + 1 - k, c)) for c in range(cols) for q in range(min(c + 2, cols)) for k in range(2)]
    return row_value, col_value, lax.ppermute(col_value, AXES, swap)


def body(tile, mask):
    rows = lax.axis_size("row")
    cols = lax.axis_size("col")
    at = lambda r, c: r * cols + c
    W = 2 * K
    send = lambda value, pairs: lax.ppermute(value, AXES, pairs)
    whole, left, own = local(prepare_kernel, [(W, 2 * W), (W, W), (W, W)], (mask, tile), "prepare", masks=1)
    partner = send(whole, [(at(2 * c + k, c), at(2 * c + 1 - k, c)) for c in range(cols) for k in range(2)])
    above = send(left, [(at(2 * c - 1, c), at(2 * c, c)) for c in range(1, cols)])
    right = send(left, [(at(2 * c + 1, c + 1), at(2 * c + 1, c)) for c in range(cols - 1)])
    beside = send(
        own,
        [(at(2 * c - 1, c - 1), at(2 * c, c)) for c in range(1, cols)]
        + [(at(2 * c + 2, c + 1), at(2 * c + 1, c)) for c in range(cols - 1)],
    )
    tile_late, partner, above, right, beside = lax.optimization_barrier((tile, partner, above, right, beside))
    live = [(r, c) for r in range(rows) for c in range(r // 2, cols)]
    up = send(tile_late, [(at(r, c), at(r + 1, c)) for r, c in live if r + 1 < rows])
    down = send(tile_late, [(at(r, c), at(r - 1, c)) for r, c in live if r])
    step = (4 * K, W)
    row_step, col_step = local(
        steps_kernel,
        [step, step],
        (mask, tile, partner, above, right, beside),
        "steps",
        scratch=(pltpu.VMEM((3, W, W), jnp.float32), pltpu.VMEM((2, W, W), jnp.float32)),
        masks=1,
    )
    row_step, mine, other = trees(row_step, col_step, cols)
    left_half, right_half = local(rows_kernel, [(W, W), (W, W)], (row_step, up, tile, down), "rows")
    full = [(r, c) for r in range(rows) for c in range(max((r - 1) // 2, 0), cols)]
    before = send(right_half, [(at(r, c), at(r, c + 1)) for r, c in full if c + 1 < cols])
    after = send(left_half, [(at(r, c), at(r, c - 1)) for r, c in full if c])
    return local(
        cols_kernel, [(W, 2 * W)], (mine, other, before, left_half, right_half, after), "cols"
    )[0]


def solution(mesh):
    placed = (P("row", "col"), P(None, "row"))
    return jax.shard_map(
        body, mesh=mesh, in_specs=placed, out_specs=P("row", "col"), check_vma=False
    )
```

```python
import jax
import jax.numpy as jnp
from jax import lax
from jax.experimental import pallas as pl
from jax.experimental.pallas import tpu as pltpu
from jax.sharding import PartitionSpec as P

K = 128


AXES = ("row", "col")


NN=((1,),(0,)); NT=((1,),(1,))


def halves(x):
    hi = x.astype(jnp.bfloat16)
    return hi, (x - hi.astype(jnp.float32)).astype(jnp.bfloat16)


def dot1(a, b, dims):
    return lax.dot_general(a, b, (dims, ((), ())), preferred_element_type=jnp.float32)


def mm(a, b, dims=NN):
    ah, al = halves(a); bh, bl = halves(b)
    return dot1(ah, bh, dims) + (dot1(ah, bl, dims) + dot1(al, bh, dims))


def mlow(a, b, dims=NN):
    return dot1(a.astype(jnp.bfloat16), b.astype(jnp.bfloat16), dims)


def grids():
    i = lax.broadcasted_iota(jnp.int32, (K, K), 0)
    j = lax.broadcasted_iota(jnp.int32, (K, K), 1)
    return (i == j).astype(jnp.float32), jnp.where(i > j, 1.0, jnp.where(i == j, 0.5, 0.0))


def worst(parts):
    sums = [jnp.sum(x * x) for x in parts]
    top = sums[0]
    for value in sums[1:]:
        top = jnp.where(value <= top, top, value)
    return top


def fast_inverse_cholesky(s_list, eye, phi):
    ws = []
    for s in s_list:
        d = s * eye
        dr = lax.rsqrt(jnp.sum(d, axis=0, keepdims=True)); dc = lax.rsqrt(jnp.sum(d, axis=1, keepdims=True))
        ws.append((s * dc * dr - eye, dr))
    ps = [phi * e for e, _ in ws]
    qs = [mlow(p, p, NT) for p in ps]
    ps = [phi * (e - q) for (e, _), q in zip(ws, qs)]
    qs = [mlow(p, p) for p in ps]
    w = [(eye - p + q) * dr for p, q, (_, dr) in zip(ps, qs, ws)]
    for last in range(2):
        dot = mm if last else mlow
        t = [dot(a, s) for a, s in zip(w, s_list)]
        e = [dot(a, b, NT) - eye for a, b in zip(t, w)]
        u = [dot(phi * b, a) for a, b in zip(w, e)]
        w = [a - b for a, b in zip(w, u)]
    return w, worst(e)


def fast_inverse(a_list, eye):
    cs = [K / jnp.sum(a * eye) for a in a_list]
    r = [eye - a * c for a, c in zip(a_list, cs)]
    r2 = [mm(x, x) for x in r]
    pa = [eye + x for x in r]
    r4 = [mm(x, x) for x in r2]
    pa = [p + mm(q, p) for p, q in zip(pa, r2)]
    return [(p + mm(q, p)) * c for p, q, c in zip(pa, r4, cs)], worst(r4)


def finish(m, c, nop):
    x = [mm(a, b) for a, b in zip(m, c)]
    t = [mm(a, b) for a, b in zip(x, nop)]
    m2 = [mm(a, a) for a in m]
    n2 = [mm(a, a) for a in nop]
    x = [a + mm(b, q) for a, b, q in zip(x, m, t)]
    t = [mm(a, b) for a, b in zip(x, n2)]
    return [a + mm(b, q) for a, b, q in zip(x, m2, t)]


def direct_inverse_cholesky(s):
    i = lax.broadcasted_iota(jnp.int32, (K, K), 0)
    i2 = lax.broadcasted_iota(jnp.int32, (K, 2 * K), 0)
    j2 = lax.broadcasted_iota(jnp.int32, (K, 2 * K), 1)
    t0 = jnp.concatenate([s, (i == lax.broadcasted_iota(jnp.int32, (K, K), 1)).astype(jnp.float32)], axis=1)

    def step(j, t):
        row = jnp.sum(jnp.where(i2 == j, t, 0.0), axis=0, keepdims=True)
        col = jnp.sum(jnp.where(j2 == j, t, 0.0), axis=1, keepdims=True)
        piv = jnp.sum(jnp.where(j2[:1] == j, row, 0.0), axis=1, keepdims=True)
        new = row * lax.rsqrt(piv)
        t = t - jnp.where(i2 > j, col * lax.rsqrt(piv), 0.0) * new
        return jnp.where(i2 == j, new, t)

    return lax.fori_loop(0, K, step, t0)[:, K:]


def pair_factors(a_list, c_list, b_list, out_refs, flags, parts=None):
    eye, phi = grids()
    shifts = [jnp.sum(b * eye) / K for b in b_list]
    on = [f > 0 for f in flags]
    a_s = [jnp.where(f, a - s * eye, eye) for f, a, s in zip(on, a_list, shifts)]
    c_list = [jnp.where(f, c, 0.0) for f, c in zip(on, c_list)]
    nop = [jnp.where(f, b - s * eye, 0.0) for f, b, s in zip(on, b_list, shifts)]
    m, e0 = fast_inverse(a_s, eye)

    def rest(m, chol):
        x = finish(m, c_list, nop)
        xt = [v.T for v in x]
        grams = [eye + mm(v, v, NT) for v in xt] + [eye + mm(v, v, NT) for v in x]
        w, e1 = chol(grams)
        n = len(x)
        for p in range(n):
            w1, w2 = w[p], w[n + p]
            keep = on[p]
            out_refs[p][:K, :K] = jnp.where(keep, -mm(w1, xt[p]), eye)
            out_refs[p][:K, K:] = jnp.where(keep, w1, 0.0)
            out_refs[p][K:, :K] = jnp.where(keep, w2, 0.0)
            out_refs[p][K:, K:] = jnp.where(keep, mm(w2, x[p]), eye)
            if parts is not None:
                parts[p, 0] = jnp.where(keep, x[p], eye)
                parts[p, 1] = jnp.where(keep, w1, -eye)
                parts[p, 2] = jnp.where(keep, w2, eye)
        return e1

    e1 = rest(m, lambda g: fast_inverse_cholesky(g, eye, phi))
    good = jnp.logical_and(e0 < 1e-5, e1 < 6e-3)

    @pl.when(jnp.logical_not(good))
    def _():
        inv = []
        for a in a_s:
            at = a.T
            w = direct_inverse_cholesky(mm(at, at, NT))
            inv.append(mm(mm(w.T, w.T, NT), at))
        rest(inv, lambda g: ([direct_inverse_cholesky(v) for v in g], jnp.float32(0)))


def pick(odd, when_odd, when_even):
    return jnp.where(odd, when_odd, when_even)


def prepare_kernel(mask_ref, tile_ref, whole_ref, left_ref, own_ref):
    odd = lax.axis_index("row") % 2 == 1
    i = lax.broadcasted_iota(jnp.int32, (8, K), 0)
    j = lax.broadcasted_iota(jnp.int32, (8, K), 1)
    first = (mask_ref[0, 0] > 0).astype(jnp.float32)
    second = (mask_ref[1, 0] > 0).astype(jnp.float32)
    flags = jnp.where(j == 0, jnp.where(i == 7, first, jnp.where(i == 6, second, 0.0)), 0.0)
    whole_ref[...] = tile_ref[...]
    whole_ref[2 * K - 8 :, :K] = flags
    left_ref[...] = tile_ref[:, : 2 * K]
    own_ref[...] = pick(odd, tile_ref[:, 2 * K :], tile_ref[:, : 2 * K])
    own_ref[2 * K - 8 :, :K] = flags


def flags_of(ref):
    corner = ref[2 * K - 8 :, :K]
    i = lax.broadcasted_iota(jnp.int32, (8, K), 0)
    return jnp.sum(jnp.where(i == 7, corner, 0.0)) > 0.5, jnp.sum(jnp.where(i == 6, corner, 0.0)) > 0.5


def steps_kernel(mask_ref, tile_ref, partner_ref, above_ref, right_ref, next_ref, row_ref, col_ref, f1, f2, parts):
    row = lax.axis_index("row")
    col = lax.axis_index("col")
    odd = row % 2 == 1
    owner = col == row // 2

    @pl.when(jnp.logical_not(owner))
    def _():
        row_ref[...] = jnp.zeros_like(row_ref)
        col_ref[...] = jnp.zeros_like(col_ref)

    @pl.when(owner)
    def _():
        W = 2 * K
        d0 = lambda i, j: pick(odd, tile_ref[i, W + j.start : W + j.stop], tile_ref[i, j])
        dm = lambda i, j: pick(odd, partner_ref[i, j], next_ref[i, j])
        dp = lambda i, j: pick(odd, next_ref[i, j], partner_ref[i, W + j.start : W + j.stop])
        lo, hi = slice(0, K), slice(K, W)
        partner1, partner2 = flags_of(partner_ref)
        next1, next2 = flags_of(next_ref)
        odd_i = odd.astype(jnp.int32)
        p1, p2, n1, n2 = [v.astype(jnp.int32) for v in (partner1, partner2, next1, next2)]
        m_flag = odd_i * p1 + (1 - odd_i) * n1
        m_flag2 = odd_i * p2 + (1 - odd_i) * n2
        p_flag = odd_i * n1 + (1 - odd_i) * p1
        blocks = (dm, d0, dp)
        pair_factors(
            [d(lo, lo) for d in blocks],
            [d(lo, hi) for d in blocks],
            [d(hi, hi) for d in blocks],
            [f1.at[p] for p in range(3)],
            [m_flag, mask_ref[0, 0], p_flag],
            parts,
        )

        def congruent(f, d):
            left, right = f[:, :K], f[:, K:]
            g = jnp.concatenate([mm(left, d(lo, lo)), mm(left, d(lo, hi)) + mm(right, d(hi, hi))], axis=1)
            return mm(g, f, NT)

        am = pick(odd, partner_ref[:, W:], above_ref[...])
        a0 = pick(odd, right_ref[...], tile_ref[:, W:])
        fm_low, f0_top, f0_low, fp_top = f1[0, K:, :], f1[1, :K, :], f1[1, K:, :], f1[2, :K, :]
        pair_factors(
            [congruent(fm_low, dm), congruent(f0_low, d0)],
            [mm(mm(fm_low, am), f0_top, NT), mm(mm(f0_low, a0), fp_top, NT)],
            [congruent(f0_top, d0), congruent(fp_top, dp)],
            [f2.at[p] for p in range(2)],
            [m_flag2, mask_ref[1, 0]],
        )
        eye, phi = grids()
        low = phi > 0.25

        def packed(lower, second):
            return jnp.where(low, lower, second.T), jnp.sum(second * eye, axis=0, keepdims=True)

        fm_x, f0_x, fp_x = parts[0, 0], parts[1, 0], parts[2, 0]
        z2 = mm(f2[0, K:, K:], parts[1, 1])
        z3 = mm(f2[1, :K, :K], parts[1, 2])
        row_y, row_diag = packed(mm(f2[0, K:, :K], parts[0, 2]), mm(f2[1, :K, K:], parts[2, 1]))
        col_y, col_diag = packed(mm(f2[1, K:, :K], parts[1, 2]), mm(f2[0, :K, K:], parts[1, 1]))
        i = lax.broadcasted_iota(jnp.int32, (8, K), 0)
        am_, a0_, ap_ = [(f > 0).astype(jnp.float32) for f in (m_flag, mask_ref[0, 0], p_flag)]
        for out, values, diag, marks in (
            (row_ref, (fm_x, f0_x, fp_x, z2, z3, row_y), row_diag, (am_, a0_, ap_)),
            (col_ref, (f0_x, z2, z3, col_y), col_diag, (a0_,)),
        ):
            for n, value in enumerate(values):
                out[n * K : (n + 1) * K, :] = value
            tail = jnp.where(i == 0, diag, 0.0)
            for n, mark in enumerate(marks):
                tail = jnp.where(i == n + 1, mark, tail)
            out[len(values) * K :, :] = tail


def unpacked(both, tail):
    eye, phi = grids()
    low = phi > 0.25
    return jnp.where(low, both, 0.0), jnp.where(low, 0.0, both).T + eye * tail[0:1, :]


def rows_kernel(step_ref, up_ref, own_ref, down_ref, out_ref):
    xm, x0, xp, z2, z3, both = [step_ref[n * K : (n + 1) * K, :] for n in range(6)]
    tail = step_ref[6 * K :, :]
    y1, y4 = unpacked(both, tail)
    am, a0, ap = [tail[n : n + 1, :1] for n in (1, 2, 3)]
    x0t, xpt = x0.T, xp.T
    own_top, own_low = own_ref[:K, :], own_ref[K:, :]
    t1 = am * up_ref[:K, :] + mm(xm, up_ref[K:, :])
    t2 = a0 * own_low - mm(x0t, own_top)
    t3 = a0 * own_top + mm(x0, own_low)
    t4 = ap * down_ref[K:, :] - mm(xpt, down_ref[:K, :])
    out_ref[:K, :] = mm(y1, t1) + mm(z2, t2)
    out_ref[K:, :] = mm(z3, t3) + mm(y4, t4)


def col_parts(mine_ref, other_ref):
    odd = lax.axis_index("row") % 2 == 1
    mine, other = mine_ref[...], other_ref[...]
    for message in (pick(odd, other, mine), pick(odd, mine, other)):
        x, z2, z3, both = [message[n * K : (n + 1) * K, :] for n in range(4)]
        tail = message[4 * K :, :]
        y1, y4 = unpacked(both, tail)
        yield x, z2, z3, y1, y4, tail[1:2, :1]


def edges_kernel(mine_ref, other_ref, rows_ref, to_left_ref, to_right_ref):
    (xe, _, _, _, y4e, ae), (xo, _, _, y1o, _, ao) = col_parts(mine_ref, other_ref)
    le, re, lo, ro = [rows_ref[:, n * K : (n + 1) * K] for n in range(4)]
    to_left_ref[...] = mm(ae * re - mm(le, xe), y4e, NT)
    to_right_ref[...] = mm(ao * lo + mm(ro, xo, NT), y1o, NT)


def inner_kernel(mine_ref, other_ref, rows_ref, out_ref):
    (xe, z2e, z3e, y1e, _, ae), (xo, z2o, z3o, _, y4o, ao) = col_parts(mine_ref, other_ref)
    le, re, lo, ro = [rows_ref[:, n * K : (n + 1) * K] for n in range(4)]
    ue = ae * re - mm(le, xe)
    ve = ae * le + mm(re, xe, NT)
    uo = ao * ro - mm(lo, xo)
    vo = ao * lo + mm(ro, xo, NT)
    out_ref[:, :K] = mm(ue, z2e, NT)
    out_ref[:, K : 2 * K] = mm(ve, z3e, NT) + mm(uo, y4o, NT)
    out_ref[:, 2 * K : 3 * K] = mm(uo, z2o, NT) + mm(ve, y1e, NT)
    out_ref[:, 3 * K :] = mm(vo, z3o, NT)


def local(kernel, shapes, args, scratch=(), masks=0):
    smem = pl.BlockSpec(memory_space=pltpu.SMEM)
    vmem = pl.BlockSpec(memory_space=pltpu.VMEM)
    return pl.pallas_call(
        kernel,
        out_shape=[jax.ShapeDtypeStruct(shape, jnp.float32) for shape in shapes],
        in_specs=[smem] * masks + [vmem] * (len(args) - masks),
        out_specs=[vmem] * len(shapes),
        scratch_shapes=list(scratch),
    )(*args)


def trees(row_value, col_value, cols):
    at = lambda r, c: r * cols + c
    row_lists = [
        [at(r, c) for c in range(r // 2, cols)] + ([at(r, r // 2 - 1)] if r % 2 == 0 and r else [])
        for r in range(2 * cols)
    ]
    col_lists = [
        [at(2 * q + k, c) for q in range(c, -1, -1)] + ([at(2 * c + 2 + k, c)] if c + 1 < cols else [])
        for k in range(2)
        for c in range(cols)
    ]
    orders = ((8, 4, 2, 1), (1, 8, 4, 2))
    sources = [[0], [0]]

    def pairs(lists, core, i):
        step = orders[core][i]
        return [(line[s], line[s + step]) for line in lists for s in sources[core] if s + step < len(line)]

    for i in range(4):
        row_in = lax.ppermute(row_value, AXES, pairs(row_lists[::2], 0, i) + pairs(row_lists[1::2], 1, i))
        col_in = lax.ppermute(col_value, AXES, pairs(col_lists[:cols], 0, i) + pairs(col_lists[cols:], 1, i))
        row_value, col_value = lax.optimization_barrier((row_value + row_in, col_value + col_in))
        sources = [s + [v + orders[k][i] for v in s] for k, s in enumerate(sources)]
    swap = [(at(2 * q + k, c), at(2 * q + 1 - k, c)) for c in range(cols) for q in range(min(c + 2, cols)) for k in range(2)]
    return row_value, col_value, lax.ppermute(col_value, AXES, swap)


def body(tile, mask):
    rows = lax.axis_size("row")
    cols = lax.axis_size("col")
    at = lambda r, c: r * cols + c
    W = 2 * K
    send = lambda value, pairs: lax.ppermute(value, AXES, pairs)
    whole, left, own = local(prepare_kernel, [(W, 2 * W), (W, W), (W, W)], (mask, tile), masks=1)
    partner = send(whole, [(at(2 * c + k, c), at(2 * c + 1 - k, c)) for c in range(cols) for k in range(2)])
    above = send(left, [(at(2 * c - 1, c), at(2 * c, c)) for c in range(1, cols)])
    right = send(left, [(at(2 * c + 1, c + 1), at(2 * c + 1, c)) for c in range(cols - 1)])
    beside = send(
        own,
        [(at(2 * c - 1, c - 1), at(2 * c, c)) for c in range(1, cols)]
        + [(at(2 * c + 2, c + 1), at(2 * c + 1, c)) for c in range(cols - 1)],
    )
    tile_late, partner, above, right, beside = lax.optimization_barrier((tile, partner, above, right, beside))
    live = [(r, c) for r in range(rows) for c in range(r // 2, cols)]
    up = send(tile_late, [(at(r, c), at(r + 1, c)) for r, c in live if r + 1 < rows])
    down = send(tile_late, [(at(r, c), at(r - 1, c)) for r, c in live if r])
    row_step, col_step = local(
        steps_kernel,
        [(6 * K + 8, K), (4 * K + 8, K)],
        (mask, tile, partner, above, right, beside),
        scratch=(
            pltpu.VMEM((3, W, W), jnp.float32),
            pltpu.VMEM((2, W, W), jnp.float32),
            pltpu.VMEM((3, 3, K, K), jnp.float32),
        ),
        masks=1,
    )
    row_step, mine, other = trees(row_step, col_step, cols)
    done_rows = local(rows_kernel, [(W, 2 * W)], (row_step, up, tile, down))[0]
    to_left, to_right = local(edges_kernel, [(W, K), (W, K)], (mine, other, done_rows))
    full = [(r, c) for r in range(rows) for c in range(max((r - 1) // 2, 0), cols)]
    before = send(to_right, [(at(r, c), at(r, c + 1)) for r, c in full if c + 1 < cols])
    after = send(to_left, [(at(r, c), at(r, c - 1)) for r, c in full if c])
    inner = local(inner_kernel, [(W, 2 * W)], (mine, other, done_rows))[0]
    return jnp.concatenate([inner[:, :K] + before, inner[:, K : 3 * K], inner[:, 3 * K :] + after], axis=1)


def solution(mesh):
    placed = (P("row", "col"), P(None, "row"))
    return jax.shard_map(body, mesh=mesh, in_specs=placed, out_specs=P("row", "col"), check_vma=False)
```

```python
import jax
import jax.numpy as jnp
from jax import lax
from jax.experimental import pallas as pl
from jax.experimental.pallas import tpu as pltpu
from jax.sharding import PartitionSpec as P

K = 128


AXES = ("row", "col")


NN=((1,),(0,)); NT=((1,),(1,))


def halves(x):
    hi = x.astype(jnp.bfloat16)
    return hi, (x - hi.astype(jnp.float32)).astype(jnp.bfloat16)


def dot1(a, b, dims):
    return lax.dot_general(a, b, (dims, ((), ())), preferred_element_type=jnp.float32)


def mm(a, b, dims=NN):
    ah, al = halves(a); bh, bl = halves(b)
    return dot1(ah, bh, dims) + (dot1(ah, bl, dims) + dot1(al, bh, dims))


def mlow(a, b, dims=NN):
    return dot1(a.astype(jnp.bfloat16), b.astype(jnp.bfloat16), dims)


def grids():
    i = lax.broadcasted_iota(jnp.int32, (K, K), 0)
    j = lax.broadcasted_iota(jnp.int32, (K, K), 1)
    return (i == j).astype(jnp.float32), jnp.where(i > j, 1.0, jnp.where(i == j, 0.5, 0.0))


def worst(parts):
    sums = [jnp.sum(x * x) for x in parts]
    top = sums[0]
    for value in sums[1:]:
        top = jnp.where(value <= top, top, value)
    return top


def fast_inverse_cholesky(s_list, eye, phi):
    ws = []
    for s in s_list:
        d = s * eye
        dr = lax.rsqrt(jnp.sum(d, axis=0, keepdims=True)); dc = lax.rsqrt(jnp.sum(d, axis=1, keepdims=True))
        ws.append((s * dc * dr - eye, dr))
    ps = [phi * e for e, _ in ws]
    qs = [mlow(p, p, NT) for p in ps]
    ps = [phi * (e - q) for (e, _), q in zip(ws, qs)]
    qs = [mlow(p, p) for p in ps]
    w = [(eye - p + q) * dr for p, q, (_, dr) in zip(ps, qs, ws)]
    for last in range(2):
        dot = mm if last else mlow
        t = [dot(a, s) for a, s in zip(w, s_list)]
        e = [dot(a, b, NT) - eye for a, b in zip(t, w)]
        u = [dot(phi * b, a) for a, b in zip(w, e)]
        w = [a - b for a, b in zip(w, u)]
    return w, worst(e)


def fast_inverse(a_list, eye):
    cs = [K / jnp.sum(a * eye) for a in a_list]
    r = [eye - a * c for a, c in zip(a_list, cs)]
    r2 = [mm(x, x) for x in r]
    pa = [eye + x for x in r]
    r4 = [mm(x, x) for x in r2]
    pa = [p + mm(q, p) for p, q in zip(pa, r2)]
    return [(p + mm(q, p)) * c for p, q, c in zip(pa, r4, cs)], worst(r4)


def finish(m, c, nop):
    x = [mm(a, b) for a, b in zip(m, c)]
    t = [mm(a, b) for a, b in zip(x, nop)]
    m2 = [mm(a, a) for a in m]
    n2 = [mm(a, a) for a in nop]
    x = [a + mm(b, q) for a, b, q in zip(x, m, t)]
    t = [mm(a, b) for a, b in zip(x, n2)]
    return [a + mm(b, q) for a, b, q in zip(x, m2, t)]


def direct_inverse_cholesky(s):
    i = lax.broadcasted_iota(jnp.int32, (K, K), 0)
    i2 = lax.broadcasted_iota(jnp.int32, (K, 2 * K), 0)
    j2 = lax.broadcasted_iota(jnp.int32, (K, 2 * K), 1)
    t0 = jnp.concatenate([s, (i == lax.broadcasted_iota(jnp.int32, (K, K), 1)).astype(jnp.float32)], axis=1)

    def step(j, t):
        row = jnp.sum(jnp.where(i2 == j, t, 0.0), axis=0, keepdims=True)
        col = jnp.sum(jnp.where(j2 == j, t, 0.0), axis=1, keepdims=True)
        piv = jnp.sum(jnp.where(j2[:1] == j, row, 0.0), axis=1, keepdims=True)
        new = row * lax.rsqrt(piv)
        t = t - jnp.where(i2 > j, col * lax.rsqrt(piv), 0.0) * new
        return jnp.where(i2 == j, new, t)

    return lax.fori_loop(0, K, step, t0)[:, K:]


def pair_factors(a_list, c_list, b_list, out_refs, flags, parts=None):
    eye, phi = grids()
    shifts = [jnp.sum(b * eye) / K for b in b_list]
    on = [f > 0 for f in flags]
    a_s = [jnp.where(f, a - s * eye, eye) for f, a, s in zip(on, a_list, shifts)]
    c_list = [jnp.where(f, c, 0.0) for f, c in zip(on, c_list)]
    nop = [jnp.where(f, b - s * eye, 0.0) for f, b, s in zip(on, b_list, shifts)]
    m, e0 = fast_inverse(a_s, eye)

    def rest(m, chol):
        x = finish(m, c_list, nop)
        xt = [v.T for v in x]
        grams = [eye + mm(v, v, NT) for v in xt] + [eye + mm(v, v, NT) for v in x]
        w, e1 = chol(grams)
        n = len(x)
        for p in range(n):
            w1, w2 = w[p], w[n + p]
            keep = on[p]
            out_refs[p][:K, :K] = jnp.where(keep, -mm(w1, xt[p]), eye)
            out_refs[p][:K, K:] = jnp.where(keep, w1, 0.0)
            out_refs[p][K:, :K] = jnp.where(keep, w2, 0.0)
            out_refs[p][K:, K:] = jnp.where(keep, mm(w2, x[p]), eye)
            if parts is not None:
                parts[p, 0] = jnp.where(keep, x[p], eye)
                parts[p, 1] = jnp.where(keep, w1, -eye)
                parts[p, 2] = jnp.where(keep, w2, eye)
        return e1

    e1 = rest(m, lambda g: fast_inverse_cholesky(g, eye, phi))
    good = jnp.logical_and(e0 < 1e-5, e1 < 6e-3)

    @pl.when(jnp.logical_not(good))
    def _():
        inv = []
        for a in a_s:
            at = a.T
            w = direct_inverse_cholesky(mm(at, at, NT))
            inv.append(mm(mm(w.T, w.T, NT), at))
        rest(inv, lambda g: ([direct_inverse_cholesky(v) for v in g], jnp.float32(0)))


def pick(odd, when_odd, when_even):
    return jnp.where(odd, when_odd, when_even)


def prepare_kernel(mask_ref, tile_ref, own_ref, coupling_ref):
    odd = lax.axis_index("row") % 2 == 1
    i = lax.broadcasted_iota(jnp.int32, (8, K), 0)
    j = lax.broadcasted_iota(jnp.int32, (8, K), 1)
    marks = (mask_ref[...] > 0).astype(jnp.float32)
    flags = jnp.where(j == 0, jnp.where(i == 7, marks[0:1, :], jnp.where(i == 6, marks[1:2, :], 0.0)), 0.0)
    own_ref[...] = pick(odd, tile_ref[:, 2 * K :], tile_ref[:, : 2 * K])
    own_ref[2 * K - 8 :, :K] = flags
    coupling_ref[...] = pick(odd, tile_ref[:, : 2 * K], tile_ref[:, 2 * K :])


def flags_of(ref):
    corner = ref[2 * K - 8 :, :K]
    i = lax.broadcasted_iota(jnp.int32, (8, K), 0)
    return jnp.sum(jnp.where(i == 7, corner, 0.0)) > 0.5, jnp.sum(jnp.where(i == 6, corner, 0.0)) > 0.5


def steps_kernel(own_ref, coupling_ref, partner_ref, beside_ref, near_ref, right_ref, row_ref, col_ref, f1, f2, parts):
    row = lax.axis_index("row")
    col = lax.axis_index("col")
    odd = row % 2 == 1
    owner = col == row // 2

    @pl.when(jnp.logical_not(owner))
    def _():
        row_ref[...] = jnp.zeros_like(row_ref)
        col_ref[...] = jnp.zeros_like(col_ref)

    @pl.when(owner)
    def _():
        W = 2 * K
        d0 = lambda i, j: own_ref[i, j]
        dm = lambda i, j: pick(odd, partner_ref[i, j], beside_ref[i, j])
        dp = lambda i, j: pick(odd, beside_ref[i, j], partner_ref[i, j])
        lo, hi = slice(0, K), slice(K, W)
        odd_i = odd.astype(jnp.int32)
        own1, own2, p1, p2, n1, n2 = [
            v.astype(jnp.int32) for ref in (own_ref, partner_ref, beside_ref) for v in flags_of(ref)
        ]
        m_flag = odd_i * p1 + (1 - odd_i) * n1
        m_flag2 = odd_i * p2 + (1 - odd_i) * n2
        p_flag = odd_i * n1 + (1 - odd_i) * p1
        blocks = (dm, d0, dp)
        pair_factors(
            [d(lo, lo) for d in blocks],
            [d(lo, hi) for d in blocks],
            [d(hi, hi) for d in blocks],
            [f1.at[p] for p in range(3)],
            [m_flag, own1, p_flag],
            parts,
        )

        def congruent(f, d):
            left, right = f[:, :K], f[:, K:]
            g = jnp.concatenate([mm(left, d(lo, lo)), mm(left, d(lo, hi)) + mm(right, d(hi, hi))], axis=1)
            return mm(g, f, NT)

        am = near_ref[...]
        a0 = pick(odd, right_ref[...], coupling_ref[...])
        fm_low, f0_top, f0_low, fp_top = f1[0, K:, :], f1[1, :K, :], f1[1, K:, :], f1[2, :K, :]
        pair_factors(
            [congruent(fm_low, dm), congruent(f0_low, d0)],
            [mm(mm(fm_low, am), f0_top, NT), mm(mm(f0_low, a0), fp_top, NT)],
            [congruent(f0_top, d0), congruent(fp_top, dp)],
            [f2.at[p] for p in range(2)],
            [m_flag2, own2],
        )
        eye, phi = grids()
        low = phi > 0.25

        def packed(lower, second):
            return jnp.where(low, lower, second.T), jnp.sum(second * eye, axis=0, keepdims=True)

        fm_x, f0_x, fp_x = parts[0, 0], parts[1, 0], parts[2, 0]
        z2 = mm(f2[0, K:, K:], parts[1, 1])
        z3 = mm(f2[1, :K, :K], parts[1, 2])
        row_y, row_diag = packed(mm(f2[0, K:, :K], parts[0, 2]), mm(f2[1, :K, K:], parts[2, 1]))
        col_y, col_diag = packed(mm(f2[1, K:, :K], parts[1, 2]), mm(f2[0, :K, K:], parts[1, 1]))
        i = lax.broadcasted_iota(jnp.int32, (8, K), 0)
        am_, a0_, ap_ = [(f > 0).astype(jnp.float32) for f in (m_flag, own1, p_flag)]
        for out, values, diag, marks in (
            (row_ref, (fm_x, f0_x, fp_x, z2, z3, row_y), row_diag, (am_, a0_, ap_)),
            (col_ref, (f0_x, z2, z3, col_y), col_diag, (a0_,)),
        ):
            for n, value in enumerate(values):
                out[n * K : (n + 1) * K, :] = value
            tail = jnp.where(i == 0, diag, 0.0)
            for n, mark in enumerate(marks):
                tail = jnp.where(i == n + 1, mark, tail)
            out[len(values) * K :, :] = tail


def unpacked(both, tail):
    eye, phi = grids()
    low = phi > 0.25
    return jnp.where(low, both, 0.0), jnp.where(low, 0.0, both).T + eye * tail[0:1, :]


def rows_kernel(step_ref, up_ref, own_ref, down_ref, out_ref):
    xm, x0, xp, z2, z3, both = [step_ref[n * K : (n + 1) * K, :] for n in range(6)]
    tail = step_ref[6 * K :, :]
    y1, y4 = unpacked(both, tail)
    am, a0, ap = [tail[n : n + 1, :1] for n in (1, 2, 3)]
    x0t, xpt = x0.T, xp.T
    own_top, own_low = own_ref[:K, :], own_ref[K:, :]
    t1 = am * up_ref[:K, :] + mm(xm, up_ref[K:, :])
    t2 = a0 * own_low - mm(x0t, own_top)
    t3 = a0 * own_top + mm(x0, own_low)
    t4 = ap * down_ref[K:, :] - mm(xpt, down_ref[:K, :])
    out_ref[:K, :] = mm(y1, t1) + mm(z2, t2)
    out_ref[K:, :] = mm(z3, t3) + mm(y4, t4)


def col_parts(mine_ref, other_ref):
    odd = lax.axis_index("row") % 2 == 1
    mine, other = mine_ref[...], other_ref[...]
    for message in (pick(odd, other, mine), pick(odd, mine, other)):
        x, z2, z3, both = [message[n * K : (n + 1) * K, :] for n in range(4)]
        tail = message[4 * K :, :]
        y1, y4 = unpacked(both, tail)
        yield x, z2, z3, y1, y4, tail[1:2, :1]


def edges_kernel(mine_ref, other_ref, rows_ref, to_left_ref, to_right_ref):
    (xe, _, _, _, y4e, ae), (xo, _, _, y1o, _, ao) = col_parts(mine_ref, other_ref)
    le, re, lo, ro = [rows_ref[:, n * K : (n + 1) * K] for n in range(4)]
    to_left_ref[...] = mm(ae * re - mm(le, xe), y4e, NT)
    to_right_ref[...] = mm(ao * lo + mm(ro, xo, NT), y1o, NT)


def inner_kernel(mine_ref, other_ref, rows_ref, out_ref):
    (xe, z2e, z3e, y1e, _, ae), (xo, z2o, z3o, _, y4o, ao) = col_parts(mine_ref, other_ref)
    le, re, lo, ro = [rows_ref[:, n * K : (n + 1) * K] for n in range(4)]
    ue = ae * re - mm(le, xe)
    ve = ae * le + mm(re, xe, NT)
    uo = ao * ro - mm(lo, xo)
    vo = ao * lo + mm(ro, xo, NT)
    out_ref[:, :K] = mm(ue, z2e, NT)
    out_ref[:, K : 2 * K] = mm(ve, z3e, NT) + mm(uo, y4o, NT)
    out_ref[:, 2 * K : 3 * K] = mm(uo, z2o, NT) + mm(ve, y1e, NT)
    out_ref[:, 3 * K :] = mm(vo, z3o, NT)


def local(kernel, shapes, args, scratch=()):
    vmem = pl.BlockSpec(memory_space=pltpu.VMEM)
    return pl.pallas_call(
        kernel,
        out_shape=[jax.ShapeDtypeStruct(shape, jnp.float32) for shape in shapes],
        in_specs=[vmem] * len(args),
        out_specs=[vmem] * len(shapes),
        scratch_shapes=list(scratch),
    )(*args)


def trees(row_value, col_value, cols):
    at = lambda r, c: r * cols + c
    row_lists = [
        [at(r, c) for c in range(r // 2, cols)] + ([at(r, r // 2 - 1)] if r % 2 == 0 and r else [])
        for r in range(2 * cols)
    ]
    col_lists = [
        [at(2 * q + k, c) for q in range(c, -1, -1)] + ([at(2 * c + 2 + k, c)] if c + 1 < cols else [])
        for k in range(2)
        for c in range(cols)
    ]
    turned = lambda line: line[:1] + line[:0:-1]
    row_lists[1::2] = [turned(line) for line in row_lists[1::2]]
    col_lists[cols:] = [turned(line) for line in col_lists[cols:]]
    orders = ((8, 4, 2, 1), (1, 8, 4, 2))
    sources = [[0], [0]]

    def pairs(lists, core, i):
        step = orders[core][i]
        return [(line[s], line[s + step]) for line in lists for s in sources[core] if s + step < len(line)]

    for i in range(4):
        row_in = lax.ppermute(row_value, AXES, pairs(row_lists[::2], 0, i) + pairs(row_lists[1::2], 1, i))
        col_in = lax.ppermute(col_value, AXES, pairs(col_lists[:cols], 0, i) + pairs(col_lists[cols:], 1, i))
        row_value, col_value = lax.optimization_barrier((row_value + row_in, col_value + col_in))
        sources = [s + [v + orders[k][i] for v in s] for k, s in enumerate(sources)]
    swap = [(at(2 * q + k, c), at(2 * q + 1 - k, c)) for c in range(cols) for q in range(min(c + 2, cols)) for k in range(2)]
    return row_value, col_value, lax.ppermute(col_value, AXES, swap)


def body(tile, mask):
    rows = lax.axis_size("row")
    cols = lax.axis_size("col")
    at = lambda r, c: r * cols + c
    W = 2 * K
    send = lambda value, pairs: lax.ppermute(value, AXES, pairs)
    own, coupling = local(prepare_kernel, [(W, W), (W, W)], (mask, tile))
    partner = send(own, [(at(2 * c + k, c), at(2 * c + 1 - k, c)) for c in range(cols) for k in range(2)])
    beside = send(
        own,
        [(at(2 * c - 1, c - 1), at(2 * c, c)) for c in range(1, cols)]
        + [(at(2 * c + 2, c + 1), at(2 * c + 1, c)) for c in range(cols - 1)],
    )
    near = send(
        coupling,
        [(at(2 * c, c), at(2 * c + 1, c)) for c in range(cols)]
        + [(at(2 * c - 1, c), at(2 * c, c)) for c in range(1, cols)],
    )
    right = send(coupling, [(at(2 * c + 1, c + 1), at(2 * c + 1, c)) for c in range(cols - 1)])
    live = [(r, c) for r in range(rows) for c in range(r // 2, cols)]
    up = send(tile, [(at(r, c), at(r + 1, c)) for r, c in live if r + 1 < rows])
    down = send(tile, [(at(r, c), at(r - 1, c)) for r, c in live if r])
    row_step, col_step = local(
        steps_kernel,
        [(6 * K + 8, K), (4 * K + 8, K)],
        (own, coupling, partner, beside, near, right),
        scratch=(
            pltpu.VMEM((3, W, W), jnp.float32),
            pltpu.VMEM((2, W, W), jnp.float32),
            pltpu.VMEM((3, 3, K, K), jnp.float32),
        ),
    )
    row_step, mine, other = trees(row_step, col_step, cols)
    done_rows = local(rows_kernel, [(W, 2 * W)], (row_step, up, tile, down))[0]
    to_left, to_right = local(edges_kernel, [(W, K), (W, K)], (mine, other, done_rows))
    full = [(r, c) for r in range(rows) for c in range(max((r - 1) // 2, 0), cols)]
    before = send(to_right, [(at(r, c), at(r, c + 1)) for r, c in full if c + 1 < cols])
    after = send(to_left, [(at(r, c), at(r, c - 1)) for r, c in full if c])
    inner = local(inner_kernel, [(W, 2 * W)], (mine, other, done_rows))[0]
    return jnp.concatenate([inner[:, :K] + before, inner[:, K : 3 * K], inner[:, 3 * K :] + after], axis=1)


def solution(mesh):
    placed = (P("row", "col"), P(None, "row"))
    return jax.shard_map(body, mesh=mesh, in_specs=placed, out_specs=P("row", "col"), check_vma=False)
```

```python
import jax
import jax.numpy as jnp
from jax import lax
from jax.experimental import pallas as pl
from jax.experimental.pallas import tpu as pltpu
from jax.sharding import PartitionSpec as P

K = 128


AXES = ("row", "col")


NN=((1,),(0,)); NT=((1,),(1,))


def halves(x):
    hi = x.astype(jnp.bfloat16)
    return hi, (x - hi.astype(jnp.float32)).astype(jnp.bfloat16)


def dot1(a, b, dims):
    return lax.dot_general(a, b, (dims, ((), ())), preferred_element_type=jnp.float32)


def mm(a, b, dims=NN):
    ah, al = halves(a); bh, bl = halves(b)
    return dot1(ah, bh, dims) + (dot1(ah, bl, dims) + dot1(al, bh, dims))


def mlow(a, b, dims=NN):
    return dot1(a.astype(jnp.bfloat16), b.astype(jnp.bfloat16), dims)


def grids():
    i = lax.broadcasted_iota(jnp.int32, (K, K), 0)
    j = lax.broadcasted_iota(jnp.int32, (K, K), 1)
    return (i == j).astype(jnp.float32), jnp.where(i > j, 1.0, jnp.where(i == j, 0.5, 0.0))


def worst(parts):
    sums = [jnp.sum(x * x) for x in parts]
    top = sums[0]
    for value in sums[1:]:
        top = jnp.where(value <= top, top, value)
    return top


def fast_inverse_cholesky(s_list, eye, phi):
    ws = []
    for s in s_list:
        d = s * eye
        dr = lax.rsqrt(jnp.sum(d, axis=0, keepdims=True)); dc = lax.rsqrt(jnp.sum(d, axis=1, keepdims=True))
        ws.append((s * dc * dr - eye, dr))
    ps = [phi * e for e, _ in ws]
    qs = [mlow(p, p, NT) for p in ps]
    ps = [phi * (e - q) for (e, _), q in zip(ws, qs)]
    qs = [mlow(p, p) for p in ps]
    w = [(eye - p + q) * dr for p, q, (_, dr) in zip(ps, qs, ws)]
    for last in range(2):
        dot = mm if last else mlow
        t = [dot(a, s) for a, s in zip(w, s_list)]
        e = [dot(a, b, NT) - eye for a, b in zip(t, w)]
        u = [dot(phi * b, a) for a, b in zip(w, e)]
        w = [a - b for a, b in zip(w, u)]
    return w, worst(e)


def fast_inverse(a_list, eye):
    cs = [K / jnp.sum(a * eye) for a in a_list]
    r = [eye - a * c for a, c in zip(a_list, cs)]
    r2 = [mm(x, x) for x in r]
    pa = [eye + x for x in r]
    r4 = [mm(x, x) for x in r2]
    pa = [p + mm(q, p) for p, q in zip(pa, r2)]
    return [(p + mm(q, p)) * c for p, q, c in zip(pa, r4, cs)], worst(r4)


def finish(m, c, nop):
    x = [mm(a, b) for a, b in zip(m, c)]
    t = [mm(a, b) for a, b in zip(x, nop)]
    m2 = [mm(a, a) for a in m]
    n2 = [mm(a, a) for a in nop]
    x = [a + mm(b, q) for a, b, q in zip(x, m, t)]
    t = [mm(a, b) for a, b in zip(x, n2)]
    return [a + mm(b, q) for a, b, q in zip(x, m2, t)]


def direct_inverse_cholesky(s):
    i = lax.broadcasted_iota(jnp.int32, (K, K), 0)
    i2 = lax.broadcasted_iota(jnp.int32, (K, 2 * K), 0)
    j2 = lax.broadcasted_iota(jnp.int32, (K, 2 * K), 1)
    t0 = jnp.concatenate([s, (i == lax.broadcasted_iota(jnp.int32, (K, K), 1)).astype(jnp.float32)], axis=1)

    def step(j, t):
        row = jnp.sum(jnp.where(i2 == j, t, 0.0), axis=0, keepdims=True)
        col = jnp.sum(jnp.where(j2 == j, t, 0.0), axis=1, keepdims=True)
        piv = jnp.sum(jnp.where(j2[:1] == j, row, 0.0), axis=1, keepdims=True)
        new = row * lax.rsqrt(piv)
        t = t - jnp.where(i2 > j, col * lax.rsqrt(piv), 0.0) * new
        return jnp.where(i2 == j, new, t)

    return lax.fori_loop(0, K, step, t0)[:, K:]


def pair_factors(a_list, c_list, b_list, out_refs, flags, parts=None):
    eye, phi = grids()
    shifts = [jnp.sum(b * eye) / K for b in b_list]
    on = [f > 0 for f in flags]
    a_s = [jnp.where(f, a - s * eye, eye) for f, a, s in zip(on, a_list, shifts)]
    c_list = [jnp.where(f, c, 0.0) for f, c in zip(on, c_list)]
    nop = [jnp.where(f, b - s * eye, 0.0) for f, b, s in zip(on, b_list, shifts)]
    m, e0 = fast_inverse(a_s, eye)

    def rest(m, chol):
        x = finish(m, c_list, nop)
        xt = [v.T for v in x]
        grams = [eye + mm(v, v, NT) for v in xt] + [eye + mm(v, v, NT) for v in x]
        w, e1 = chol(grams)
        n = len(x)
        for p in range(n):
            w1, w2 = w[p], w[n + p]
            keep = on[p]
            out_refs[p][:K, :K] = jnp.where(keep, -mm(w1, xt[p]), eye)
            out_refs[p][:K, K:] = jnp.where(keep, w1, 0.0)
            out_refs[p][K:, :K] = jnp.where(keep, w2, 0.0)
            out_refs[p][K:, K:] = jnp.where(keep, mm(w2, x[p]), eye)
            if parts is not None:
                parts[p, 0] = jnp.where(keep, x[p], eye)
                parts[p, 1] = jnp.where(keep, w1, -eye)
                parts[p, 2] = jnp.where(keep, w2, eye)
        return e1

    e1 = rest(m, lambda g: fast_inverse_cholesky(g, eye, phi))
    good = jnp.logical_and(e0 < 1e-5, e1 < 6e-3)

    @pl.when(jnp.logical_not(good))
    def _():
        inv = []
        for a in a_s:
            at = a.T
            w = direct_inverse_cholesky(mm(at, at, NT))
            inv.append(mm(mm(w.T, w.T, NT), at))
        rest(inv, lambda g: ([direct_inverse_cholesky(v) for v in g], jnp.float32(0)))


def pick(odd, when_odd, when_even):
    return jnp.where(odd, when_odd, when_even)


def prepare_kernel(mask_ref, tile_ref, own_ref, coupling_ref):
    odd = lax.axis_index("row") % 2 == 1
    i = lax.broadcasted_iota(jnp.int32, (8, K), 0)
    j = lax.broadcasted_iota(jnp.int32, (8, K), 1)
    marks = (mask_ref[...] > 0).astype(jnp.float32)
    flags = jnp.where(j == 0, jnp.where(i == 7, marks[:, 0:1], jnp.where(i == 6, marks[:, 1:2], 0.0)), 0.0)
    own_ref[...] = pick(odd, tile_ref[:, 2 * K :], tile_ref[:, : 2 * K])
    own_ref[2 * K - 8 :, :K] = flags
    coupling_ref[...] = pick(odd, tile_ref[:, : 2 * K], tile_ref[:, 2 * K :])


def flags_of(ref):
    corner = ref[2 * K - 8 :, :K]
    i = lax.broadcasted_iota(jnp.int32, (8, K), 0)
    return jnp.sum(jnp.where(i == 7, corner, 0.0)) > 0.5, jnp.sum(jnp.where(i == 6, corner, 0.0)) > 0.5


def steps_kernel(own_ref, coupling_ref, partner_ref, beside_ref, near_ref, right_ref, row_ref, col_ref, f1, f2, parts):
    row = lax.axis_index("row")
    col = lax.axis_index("col")
    odd = row % 2 == 1
    owner = col == row // 2

    @pl.when(jnp.logical_not(owner))
    def _():
        row_ref[...] = jnp.zeros_like(row_ref)
        col_ref[...] = jnp.zeros_like(col_ref)

    @pl.when(owner)
    def _():
        W = 2 * K
        d0 = lambda i, j: own_ref[i, j]
        dm = lambda i, j: pick(odd, partner_ref[i, j], beside_ref[i, j])
        dp = lambda i, j: pick(odd, beside_ref[i, j], partner_ref[i, j])
        lo, hi = slice(0, K), slice(K, W)
        odd_i = odd.astype(jnp.int32)
        own1, own2, p1, p2, n1, n2 = [
            v.astype(jnp.int32) for ref in (own_ref, partner_ref, beside_ref) for v in flags_of(ref)
        ]
        m_flag = odd_i * p1 + (1 - odd_i) * n1
        m_flag2 = odd_i * p2 + (1 - odd_i) * n2
        p_flag = odd_i * n1 + (1 - odd_i) * p1
        blocks = (dm, d0, dp)
        pair_factors(
            [d(lo, lo) for d in blocks],
            [d(lo, hi) for d in blocks],
            [d(hi, hi) for d in blocks],
            [f1.at[p] for p in range(3)],
            [m_flag, own1, p_flag],
            parts,
        )

        def congruent(f, d):
            left, right = f[:, :K], f[:, K:]
            g = jnp.concatenate([mm(left, d(lo, lo)), mm(left, d(lo, hi)) + mm(right, d(hi, hi))], axis=1)
            return mm(g, f, NT)

        am = near_ref[...]
        a0 = pick(odd, right_ref[...], coupling_ref[...])
        fm_low, f0_top, f0_low, fp_top = f1[0, K:, :], f1[1, :K, :], f1[1, K:, :], f1[2, :K, :]
        pair_factors(
            [congruent(fm_low, dm), congruent(f0_low, d0)],
            [mm(mm(fm_low, am), f0_top, NT), mm(mm(f0_low, a0), fp_top, NT)],
            [congruent(f0_top, d0), congruent(fp_top, dp)],
            [f2.at[p] for p in range(2)],
            [m_flag2, own2],
        )
        eye, phi = grids()
        low = phi > 0.25

        def packed(lower, second):
            return jnp.where(low, lower, second.T), jnp.sum(second * eye, axis=0, keepdims=True)

        fm_x, f0_x, fp_x = parts[0, 0], parts[1, 0], parts[2, 0]
        z2 = mm(f2[0, K:, K:], parts[1, 1])
        z3 = mm(f2[1, :K, :K], parts[1, 2])
        row_y, row_diag = packed(mm(f2[0, K:, :K], parts[0, 2]), mm(f2[1, :K, K:], parts[2, 1]))
        col_y, col_diag = packed(mm(f2[1, K:, :K], parts[1, 2]), mm(f2[0, :K, K:], parts[1, 1]))
        i = lax.broadcasted_iota(jnp.int32, (8, K), 0)
        am_, a0_, ap_ = [(f > 0).astype(jnp.float32) for f in (m_flag, own1, p_flag)]
        for out, values, diag, marks in (
            (row_ref, (fm_x, f0_x, fp_x, z2, z3, row_y), row_diag, (a0_, am_, ap_)),
            (col_ref, (f0_x, z2, z3, col_y), col_diag, (a0_,)),
        ):
            for n, value in enumerate(values):
                out[n * K : (n + 1) * K, :] = value
            tail = jnp.where(i == 0, diag, 0.0)
            for n, mark in enumerate(marks):
                tail = jnp.where(i == n + 1, mark, tail)
            out[len(values) * K :, :] = tail


def unpacked(both, tail):
    eye, phi = grids()
    low = phi > 0.25
    return jnp.where(low, both, 0.0), jnp.where(low, 0.0, both).T + eye * tail[0:1, :]


def col_parts(mine_ref, other_ref):
    odd = lax.axis_index("row") % 2 == 1
    mine, other = mine_ref[...], other_ref[...]
    for message in (pick(odd, other, mine), pick(odd, mine, other)):
        x, z2, z3, both = [message[n * K : (n + 1) * K, :] for n in range(4)]
        tail = message[4 * K :, :]
        y1, y4 = unpacked(both, tail)
        yield x, z2, z3, y1, y4, tail[1:2, :1]


def rows_kernel(
    step_ref, up_ref, own_ref, down_ref, mine_ref, other_ref, out_ref, to_left_ref, to_right_ref
):
    xm, x0, xp, z2, z3, both = [step_ref[n * K : (n + 1) * K, :] for n in range(6)]
    tail = step_ref[6 * K :, :]
    y1, y4 = unpacked(both, tail)
    a0, am, ap = [tail[n : n + 1, :1] for n in (1, 2, 3)]
    x0t, xpt = x0.T, xp.T
    own_top, own_low = own_ref[:K, :], own_ref[K:, :]
    t1 = am * up_ref[:K, :] + mm(xm, up_ref[K:, :])
    t2 = a0 * own_low - mm(x0t, own_top)
    t3 = a0 * own_top + mm(x0, own_low)
    t4 = ap * down_ref[K:, :] - mm(xpt, down_ref[:K, :])
    out_ref[:K, :] = mm(y1, t1) + mm(z2, t2)
    out_ref[K:, :] = mm(z3, t3) + mm(y4, t4)
    (xe, _, _, _, y4e, ae), (xo, _, _, y1o, _, ao) = col_parts(mine_ref, other_ref)
    le, re, lo, ro = [out_ref[:, n * K : (n + 1) * K] for n in range(4)]
    to_left_ref[...] = mm(ae * re - mm(le, xe), y4e, NT)
    to_right_ref[...] = mm(ao * lo + mm(ro, xo, NT), y1o, NT)


def inner_kernel(mine_ref, other_ref, rows_ref, out_ref):
    (xe, z2e, z3e, y1e, _, ae), (xo, z2o, z3o, _, y4o, ao) = col_parts(mine_ref, other_ref)
    le, re, lo, ro = [rows_ref[:, n * K : (n + 1) * K] for n in range(4)]
    ue = ae * re - mm(le, xe)
    ve = ae * le + mm(re, xe, NT)
    uo = ao * ro - mm(lo, xo)
    vo = ao * lo + mm(ro, xo, NT)
    out_ref[:, :K] = mm(ue, z2e, NT)
    out_ref[:, K : 2 * K] = mm(ve, z3e, NT) + mm(uo, y4o, NT)
    out_ref[:, 2 * K : 3 * K] = mm(uo, z2o, NT) + mm(ve, y1e, NT)
    out_ref[:, 3 * K :] = mm(vo, z3o, NT)


def local(kernel, shapes, args, scratch=()):
    vmem = pl.BlockSpec(memory_space=pltpu.VMEM)
    return pl.pallas_call(
        kernel,
        out_shape=[jax.ShapeDtypeStruct(shape, jnp.float32) for shape in shapes],
        in_specs=[vmem] * len(args),
        out_specs=[vmem] * len(shapes),
        scratch_shapes=list(scratch),
    )(*args)


def trees(row_value, col_value, cols):
    at = lambda r, c: r * cols + c
    row_lists = [
        [at(r, c) for c in range(r // 2, cols)] + ([at(r, r // 2 - 1)] if r % 2 == 0 and r else [])
        for r in range(2 * cols)
    ]
    col_lists = [
        [at(2 * q + k, c) for q in range(c, -1, -1)] + ([at(2 * c + 2 + k, c)] if c + 1 < cols else [])
        for k in range(2)
        for c in range(cols)
    ]
    turned = lambda line: line[:1] + line[:0:-1]
    row_lists[1::2] = [turned(line) for line in row_lists[1::2]]
    col_lists[cols:] = [turned(line) for line in col_lists[cols:]]
    orders = ((8, 4, 2, 1), (2, 8, 4, 1))
    sources = [[0], [0]]

    def pairs(lists, core, i):
        step = orders[core][i]
        return [(line[s], line[s + step]) for line in lists for s in sources[core] if s + step < len(line)]

    for i in range(4):
        row_in = lax.ppermute(row_value, AXES, pairs(row_lists[::2], 0, i) + pairs(row_lists[1::2], 1, i))
        row_value = lax.optimization_barrier(row_value + row_in)
        col_in = lax.ppermute(col_value, AXES, pairs(col_lists[:cols], 0, i) + pairs(col_lists[cols:], 1, i))
        col_value = lax.optimization_barrier(col_value + col_in)
        sources = [s + [v + orders[k][i] for v in s] for k, s in enumerate(sources)]
    swap = [(at(2 * q + k, c), at(2 * q + 1 - k, c)) for c in range(cols) for q in range(min(c + 2, cols)) for k in range(2)]
    return row_value, col_value, lax.ppermute(col_value, AXES, swap)


def body(tile, mask):
    rows = lax.axis_size("row")
    cols = lax.axis_size("col")
    at = lambda r, c: r * cols + c
    W = 2 * K
    send = lambda value, pairs: lax.ppermute(value, AXES, pairs)
    own, coupling = local(prepare_kernel, [(W, W), (W, W)], (mask.T, tile))
    partner = send(own, [(at(2 * c + k, c), at(2 * c + 1 - k, c)) for c in range(cols) for k in range(2)])
    beside = send(
        own,
        [(at(2 * c - 1, c - 1), at(2 * c, c)) for c in range(1, cols)]
        + [(at(2 * c + 2, c + 1), at(2 * c + 1, c)) for c in range(cols - 1)],
    )
    near = send(
        coupling,
        [(at(2 * c, c), at(2 * c + 1, c)) for c in range(cols)]
        + [(at(2 * c - 1, c), at(2 * c, c)) for c in range(1, cols)],
    )
    right = send(coupling, [(at(2 * c + 1, c + 1), at(2 * c + 1, c)) for c in range(cols - 1)])
    live = [(r, c) for r in range(rows) for c in range(r // 2, cols)]
    up = send(tile, [(at(r, c), at(r + 1, c)) for r, c in live if r + 1 < rows])
    down = send(tile, [(at(r, c), at(r - 1, c)) for r, c in live if r])
    row_step, col_step = local(
        steps_kernel,
        [(6 * K + 8, K), (4 * K + 8, K)],
        (own, coupling, partner, beside, near, right),
        scratch=(
            pltpu.VMEM((3, W, W), jnp.float32),
            pltpu.VMEM((2, W, W), jnp.float32),
            pltpu.VMEM((3, 3, K, K), jnp.float32),
        ),
    )
    row_step, mine, other = trees(row_step, col_step, cols)
    full = [(r, c) for r in range(rows) for c in range(max((r - 1) // 2, 0), cols)]
    done_rows, to_left, to_right = local(
        rows_kernel, [(W, 2 * W), (W, K), (W, K)], (row_step, up, tile, down, mine, other)
    )
    before = send(to_right, [(at(r, c), at(r, c + 1)) for r, c in full if c + 1 < cols])
    after = send(to_left, [(at(r, c), at(r, c - 1)) for r, c in full if c])
    inner = local(inner_kernel, [(W, 2 * W)], (mine, other, done_rows))[0]
    return jnp.concatenate([inner[:, :K] + before, inner[:, K : 3 * K], inner[:, 3 * K :] + after], axis=1)


def solution(mesh):
    placed = (P("row", "col"), P(None, "row"))
    return jax.shard_map(body, mesh=mesh, in_specs=placed, out_specs=P("row", "col"), check_vma=False)
```

```python
import jax
import jax.numpy as jnp
from jax import lax
from jax.experimental import pallas as pl
from jax.experimental.pallas import tpu as pltpu
from jax.sharding import PartitionSpec as P

K = 128


AXES = ("row", "col")


NN=((1,),(0,)); NT=((1,),(1,))


def halves(x):
    hi = x.astype(jnp.bfloat16)
    return hi, (x - hi.astype(jnp.float32)).astype(jnp.bfloat16)


def dot1(a, b, dims):
    return lax.dot_general(a, b, (dims, ((), ())), preferred_element_type=jnp.float32)


def mm(a, b, dims=NN):
    ah, al = halves(a); bh, bl = halves(b)
    return dot1(ah, bh, dims) + (dot1(ah, bl, dims) + dot1(al, bh, dims))


def mlow(a, b, dims=NN):
    return dot1(a.astype(jnp.bfloat16), b.astype(jnp.bfloat16), dims)


def grids():
    i = lax.broadcasted_iota(jnp.int32, (K, K), 0)
    j = lax.broadcasted_iota(jnp.int32, (K, K), 1)
    return (i == j).astype(jnp.float32), jnp.where(i > j, 1.0, jnp.where(i == j, 0.5, 0.0))


def worst(parts):
    sums = [jnp.sum(x * x) for x in parts]
    top = sums[0]
    for value in sums[1:]:
        top = jnp.where(value <= top, top, value)
    return top


def fast_inverse_cholesky(s_list, eye, phi):
    ws = []
    for s in s_list:
        d = s * eye
        dr = lax.rsqrt(jnp.sum(d, axis=0, keepdims=True)); dc = lax.rsqrt(jnp.sum(d, axis=1, keepdims=True))
        ws.append((s * dc * dr - eye, dr))
    ps = [phi * e for e, _ in ws]
    qs = [mlow(p, p, NT) for p in ps]
    ps = [phi * (e - q) for (e, _), q in zip(ws, qs)]
    qs = [mlow(p, p) for p in ps]
    w = [(eye - p + q) * dr for p, q, (_, dr) in zip(ps, qs, ws)]
    for last in range(2):
        dot = mm if last else mlow
        t = [dot(a, s) for a, s in zip(w, s_list)]
        e = [dot(a, b, NT) - eye for a, b in zip(t, w)]
        u = [dot(phi * b, a) for a, b in zip(w, e)]
        w = [a - b for a, b in zip(w, u)]
    return w, worst(e)


def fast_inverse(a_list, eye):
    cs = [K / jnp.sum(a * eye) for a in a_list]
    r = [eye - a * c for a, c in zip(a_list, cs)]
    r2 = [mm(x, x) for x in r]
    pa = [eye + x for x in r]
    r4 = [mm(x, x) for x in r2]
    pa = [p + mm(q, p) for p, q in zip(pa, r2)]
    return [(p + mm(q, p)) * c for p, q, c in zip(pa, r4, cs)], worst(r4)


def finish(m, c, nop):
    x = [mm(a, b) for a, b in zip(m, c)]
    t = [mm(a, b) for a, b in zip(x, nop)]
    m2 = [mm(a, a) for a in m]
    n2 = [mm(a, a) for a in nop]
    x = [a + mm(b, q) for a, b, q in zip(x, m, t)]
    t = [mm(a, b) for a, b in zip(x, n2)]
    return [a + mm(b, q) for a, b, q in zip(x, m2, t)]


def direct_inverse_cholesky(s):
    i = lax.broadcasted_iota(jnp.int32, (K, K), 0)
    i2 = lax.broadcasted_iota(jnp.int32, (K, 2 * K), 0)
    j2 = lax.broadcasted_iota(jnp.int32, (K, 2 * K), 1)
    t0 = jnp.concatenate([s, (i == lax.broadcasted_iota(jnp.int32, (K, K), 1)).astype(jnp.float32)], axis=1)

    def step(j, t):
        row = jnp.sum(jnp.where(i2 == j, t, 0.0), axis=0, keepdims=True)
        col = jnp.sum(jnp.where(j2 == j, t, 0.0), axis=1, keepdims=True)
        piv = jnp.sum(jnp.where(j2[:1] == j, row, 0.0), axis=1, keepdims=True)
        new = row * lax.rsqrt(piv)
        t = t - jnp.where(i2 > j, col * lax.rsqrt(piv), 0.0) * new
        return jnp.where(i2 == j, new, t)

    return lax.fori_loop(0, K, step, t0)[:, K:]


def pair_factors(a_list, c_list, b_list, out_refs, flags, parts=None):
    eye, phi = grids()
    shifts = [jnp.sum(b * eye) / K for b in b_list]
    on = [f > 0 for f in flags]
    a_s = [jnp.where(f, a - s * eye, eye) for f, a, s in zip(on, a_list, shifts)]
    c_list = [jnp.where(f, c, 0.0) for f, c in zip(on, c_list)]
    nop = [jnp.where(f, b - s * eye, 0.0) for f, b, s in zip(on, b_list, shifts)]
    m, e0 = fast_inverse(a_s, eye)

    def rest(m, chol):
        x = finish(m, c_list, nop)
        xt = [v.T for v in x]
        grams = [eye + mm(v, v, NT) for v in xt] + [eye + mm(v, v, NT) for v in x]
        w, e1 = chol(grams)
        n = len(x)
        for p in range(n):
            w1, w2 = w[p], w[n + p]
            keep = on[p]
            out_refs[p][:K, :K] = jnp.where(keep, -mm(w1, xt[p]), eye)
            out_refs[p][:K, K:] = jnp.where(keep, w1, 0.0)
            out_refs[p][K:, :K] = jnp.where(keep, w2, 0.0)
            out_refs[p][K:, K:] = jnp.where(keep, mm(w2, x[p]), eye)
            if parts is not None:
                parts[p, 0] = jnp.where(keep, x[p], eye)
                parts[p, 1] = jnp.where(keep, w1, -eye)
                parts[p, 2] = jnp.where(keep, w2, eye)
        return e1

    e1 = rest(m, lambda g: fast_inverse_cholesky(g, eye, phi))
    good = jnp.logical_and(e0 < 1e-5, e1 < 6e-3)

    @pl.when(jnp.logical_not(good))
    def _():
        inv = []
        for a in a_s:
            at = a.T
            w = direct_inverse_cholesky(mm(at, at, NT))
            inv.append(mm(mm(w.T, w.T, NT), at))
        rest(inv, lambda g: ([direct_inverse_cholesky(v) for v in g], jnp.float32(0)))


def pick(odd, when_odd, when_even):
    return jnp.where(odd, when_odd, when_even)


def prepare_kernel(mask_ref, tile_ref, own_ref, coupling_ref):
    odd = lax.axis_index("row") % 2 == 1
    i = lax.broadcasted_iota(jnp.int32, (8, K), 0)
    j = lax.broadcasted_iota(jnp.int32, (8, K), 1)
    marks = (mask_ref[...] > 0).astype(jnp.float32)
    flags = jnp.where(j == 0, jnp.where(i == 7, marks[:, 0:1], jnp.where(i == 6, marks[:, 1:2], 0.0)), 0.0)
    own_ref[...] = pick(odd, tile_ref[:, 2 * K :], tile_ref[:, : 2 * K])
    own_ref[2 * K - 8 :, :K] = flags
    coupling_ref[...] = pick(odd, tile_ref[:, : 2 * K], tile_ref[:, 2 * K :])


def flags_of(ref):
    corner = ref[2 * K - 8 :, :K]
    i = lax.broadcasted_iota(jnp.int32, (8, K), 0)
    return jnp.sum(jnp.where(i == 7, corner, 0.0)) > 0.5, jnp.sum(jnp.where(i == 6, corner, 0.0)) > 0.5


def steps_kernel(own_ref, coupling_ref, partner_ref, beside_ref, near_ref, right_ref, row_ref, col_ref, f1, f2, parts):
    row = lax.axis_index("row")
    col = lax.axis_index("col")
    odd = row % 2 == 1
    owner = col == row // 2

    @pl.when(jnp.logical_not(owner))
    def _():
        row_ref[...] = jnp.zeros_like(row_ref)
        col_ref[...] = jnp.zeros_like(col_ref)

    @pl.when(owner)
    def _():
        W = 2 * K
        d0 = lambda i, j: own_ref[i, j]
        dm = lambda i, j: pick(odd, partner_ref[i, j], beside_ref[i, j])
        dp = lambda i, j: pick(odd, beside_ref[i, j], partner_ref[i, j])
        lo, hi = slice(0, K), slice(K, W)
        odd_i = odd.astype(jnp.int32)
        own1, own2, p1, p2, n1, n2 = [
            v.astype(jnp.int32) for ref in (own_ref, partner_ref, beside_ref) for v in flags_of(ref)
        ]
        m_flag = odd_i * p1 + (1 - odd_i) * n1
        m_flag2 = odd_i * p2 + (1 - odd_i) * n2
        p_flag = odd_i * n1 + (1 - odd_i) * p1
        blocks = (dm, d0, dp)
        pair_factors(
            [d(lo, lo) for d in blocks],
            [d(lo, hi) for d in blocks],
            [d(hi, hi) for d in blocks],
            [f1.at[p] for p in range(3)],
            [m_flag, own1, p_flag],
            parts,
        )

        def congruent(f, d):
            left, right = f[:, :K], f[:, K:]
            g = jnp.concatenate([mm(left, d(lo, lo)), mm(left, d(lo, hi)) + mm(right, d(hi, hi))], axis=1)
            return mm(g, f, NT)

        am = near_ref[...]
        a0 = pick(odd, right_ref[...], coupling_ref[...])
        fm_low, f0_top, f0_low, fp_top = f1[0, K:, :], f1[1, :K, :], f1[1, K:, :], f1[2, :K, :]
        pair_factors(
            [congruent(fm_low, dm), congruent(f0_low, d0)],
            [mm(mm(fm_low, am), f0_top, NT), mm(mm(f0_low, a0), fp_top, NT)],
            [congruent(f0_top, d0), congruent(fp_top, dp)],
            [f2.at[p] for p in range(2)],
            [m_flag2, own2],
        )
        eye, phi = grids()
        low = phi > 0.25

        def packed(lower, second):
            return jnp.where(low, lower, second.T), jnp.sum(second * eye, axis=0, keepdims=True)

        fm_x, f0_x, fp_x = parts[0, 0], parts[1, 0], parts[2, 0]
        z2 = mm(f2[0, K:, K:], parts[1, 1])
        z3 = mm(f2[1, :K, :K], parts[1, 2])
        row_y, row_diag = packed(mm(f2[0, K:, :K], parts[0, 2]), mm(f2[1, :K, K:], parts[2, 1]))
        col_y, col_diag = packed(mm(f2[1, K:, :K], parts[1, 2]), mm(f2[0, :K, K:], parts[1, 1]))
        i = lax.broadcasted_iota(jnp.int32, (8, K), 0)
        am_, a0_, ap_ = [(f > 0).astype(jnp.float32) for f in (m_flag, own1, p_flag)]
        for out, values, diag, marks in (
            (row_ref, (fm_x, f0_x, fp_x, z2, z3, row_y), row_diag, (a0_, am_, ap_)),
            (col_ref, (f0_x, z2, z3, col_y), col_diag, (a0_,)),
        ):
            for n, value in enumerate(values):
                out[n * K : (n + 1) * K, :] = value
            tail = jnp.where(i == 0, diag, 0.0)
            for n, mark in enumerate(marks):
                tail = jnp.where(i == n + 1, mark, tail)
            out[len(values) * K :, :] = tail


def unpacked(both, tail):
    eye, phi = grids()
    low = phi > 0.25
    return jnp.where(low, both, 0.0), jnp.where(low, 0.0, both).T + eye * tail[0:1, :]


def col_parts(mine_ref, other_ref):
    odd = lax.axis_index("row") % 2 == 1
    mine, other = mine_ref[...], other_ref[...]
    for message in (pick(odd, other, mine), pick(odd, mine, other)):
        x, z2, z3, both = [message[n * K : (n + 1) * K, :] for n in range(4)]
        tail = message[4 * K :, :]
        y1, y4 = unpacked(both, tail)
        yield x, z2, z3, y1, y4, tail[1:2, :1]


def rows_kernel(
    step_ref, up_ref, own_ref, down_ref, mine_ref, other_ref, out_ref, to_left_ref, to_right_ref
):
    xm, x0, xp, z2, z3, both = [step_ref[n * K : (n + 1) * K, :] for n in range(6)]
    tail = step_ref[6 * K :, :]
    y1, y4 = unpacked(both, tail)
    a0, am, ap = [tail[n : n + 1, :1] for n in (1, 2, 3)]
    x0t, xpt = x0.T, xp.T
    own_top, own_low = own_ref[:K, :], own_ref[K:, :]
    t1 = am * up_ref[:K, :] + mm(xm, up_ref[K:, :])
    t2 = a0 * own_low - mm(x0t, own_top)
    t3 = a0 * own_top + mm(x0, own_low)
    t4 = ap * down_ref[K:, :] - mm(xpt, down_ref[:K, :])
    out_ref[:K, :] = mm(y1, t1) + mm(z2, t2)
    out_ref[K:, :] = mm(z3, t3) + mm(y4, t4)
    (xe, _, _, _, y4e, ae), (xo, _, _, y1o, _, ao) = col_parts(mine_ref, other_ref)
    le, re, lo, ro = [out_ref[:, n * K : (n + 1) * K] for n in range(4)]
    to_left_ref[...] = mm(ae * re - mm(le, xe), y4e, NT)
    to_right_ref[...] = mm(ao * lo + mm(ro, xo, NT), y1o, NT)


def add_edges_kernel(inner_ref, before_ref, after_ref, out_ref):
    first = pl.program_id(0) == 0
    out_ref[...] = inner_ref[...] + jnp.where(first, before_ref[...], after_ref[...])


def inner_kernel(mine_ref, other_ref, rows_ref, out_ref):
    (xe, z2e, z3e, y1e, _, ae), (xo, z2o, z3o, _, y4o, ao) = col_parts(mine_ref, other_ref)
    le, re, lo, ro = [rows_ref[:, n * K : (n + 1) * K] for n in range(4)]
    ue = ae * re - mm(le, xe)
    ve = ae * le + mm(re, xe, NT)
    uo = ao * ro - mm(lo, xo)
    vo = ao * lo + mm(ro, xo, NT)
    out_ref[:, :K] = mm(ue, z2e, NT)
    out_ref[:, K : 2 * K] = mm(ve, z3e, NT) + mm(uo, y4o, NT)
    out_ref[:, 2 * K : 3 * K] = mm(uo, z2o, NT) + mm(ve, y1e, NT)
    out_ref[:, 3 * K :] = mm(vo, z3o, NT)


def local(kernel, shapes, args, scratch=()):
    vmem = pl.BlockSpec(memory_space=pltpu.VMEM)
    return pl.pallas_call(
        kernel,
        out_shape=[jax.ShapeDtypeStruct(shape, jnp.float32) for shape in shapes],
        in_specs=[vmem] * len(args),
        out_specs=[vmem] * len(shapes),
        scratch_shapes=list(scratch),
    )(*args)


def trees(row_value, col_value, cols):
    at = lambda r, c: r * cols + c
    row_lists = [
        [at(r, c) for c in range(r // 2, cols)] + ([at(r, r // 2 - 1)] if r % 2 == 0 and r else [])
        for r in range(2 * cols)
    ]
    col_lists = [
        [at(2 * q + k, c) for q in range(c, -1, -1)] + ([at(2 * c + 2 + k, c)] if c + 1 < cols else [])
        for k in range(2)
        for c in range(cols)
    ]
    turned = lambda line: line[:1] + line[:0:-1]
    row_lists[1::2] = [turned(line) for line in row_lists[1::2]]
    col_lists[cols:] = [turned(line) for line in col_lists[cols:]]
    orders = ((8, 4, 2, 1), (2, 8, 4, 1))
    sources = [[0], [0]]

    def pairs(lists, core, i):
        step = orders[core][i]
        return [(line[s], line[s + step]) for line in lists for s in sources[core] if s + step < len(line)]

    for i in range(4):
        row_in = lax.ppermute(row_value, AXES, pairs(row_lists[::2], 0, i) + pairs(row_lists[1::2], 1, i))
        row_value = lax.optimization_barrier(row_value + row_in)
        col_in = lax.ppermute(col_value, AXES, pairs(col_lists[:cols], 0, i) + pairs(col_lists[cols:], 1, i))
        col_value = lax.optimization_barrier(col_value + col_in)
        sources = [s + [v + orders[k][i] for v in s] for k, s in enumerate(sources)]
    swap = [(at(2 * q + k, c), at(2 * q + 1 - k, c)) for c in range(cols) for q in range(min(c + 2, cols)) for k in range(2)]
    return row_value, col_value, lax.ppermute(col_value, AXES, swap)


def body(tile, mask):
    rows = lax.axis_size("row")
    cols = lax.axis_size("col")
    at = lambda r, c: r * cols + c
    W = 2 * K
    send = lambda value, pairs: lax.ppermute(value, AXES, pairs)
    own, coupling = local(prepare_kernel, [(W, W), (W, W)], (mask.T, tile))
    partner = send(own, [(at(2 * c + k, c), at(2 * c + 1 - k, c)) for c in range(cols) for k in range(2)])
    beside = send(
        own,
        [(at(2 * c - 1, c - 1), at(2 * c, c)) for c in range(1, cols)]
        + [(at(2 * c + 2, c + 1), at(2 * c + 1, c)) for c in range(cols - 1)],
    )
    near = send(
        coupling,
        [(at(2 * c, c), at(2 * c + 1, c)) for c in range(cols)]
        + [(at(2 * c - 1, c), at(2 * c, c)) for c in range(1, cols)],
    )
    right = send(coupling, [(at(2 * c + 1, c + 1), at(2 * c + 1, c)) for c in range(cols - 1)])
    live = [(r, c) for r in range(rows) for c in range(r // 2, cols)]
    up = send(tile, [(at(r, c), at(r + 1, c)) for r, c in live if r + 1 < rows])
    down = send(tile, [(at(r, c), at(r - 1, c)) for r, c in live if r])
    row_step, col_step = local(
        steps_kernel,
        [(6 * K + 8, K), (4 * K + 8, K)],
        (own, coupling, partner, beside, near, right),
        scratch=(
            pltpu.VMEM((3, W, W), jnp.float32),
            pltpu.VMEM((2, W, W), jnp.float32),
            pltpu.VMEM((3, 3, K, K), jnp.float32),
        ),
    )
    row_step, mine, other = trees(row_step, col_step, cols)
    full = [(r, c) for r in range(rows) for c in range(max((r - 1) // 2, 0), cols)]
    done_rows, to_left, to_right = local(
        rows_kernel, [(W, 2 * W), (W, K), (W, K)], (row_step, up, tile, down, mine, other)
    )
    before = send(to_right, [(at(r, c), at(r, c + 1)) for r, c in full if c + 1 < cols])
    after = send(to_left, [(at(r, c), at(r, c - 1)) for r, c in full if c])
    inner = local(inner_kernel, [(W, 2 * W)], (mine, other, done_rows))[0]
    whole_edge = pl.BlockSpec((W, K), lambda i: (0, 0))
    edge = pl.BlockSpec((W, K), lambda i: (0, 3 * i))
    return pl.pallas_call(
        add_edges_kernel,
        grid=(2,),
        out_shape=jax.ShapeDtypeStruct((W, 2 * W), jnp.float32),
        in_specs=[edge, whole_edge, whole_edge],
        out_specs=edge,
        input_output_aliases={0: 0},
        name="add_edges",
    )(inner, before, after)


def solution(mesh):
    placed = (P("row", "col"), P(None, "row"))
    return jax.shard_map(body, mesh=mesh, in_specs=placed, out_specs=P("row", "col"), check_vma=False)
```
